128 devices in a mesh: row: 4 (over y), col: 4 (over x), depth: 8 (over z, core).
Axes of the slice: x: 4, y: 4, z: 4, core: 2. Of those that a mesh axis runs over, the one named last changes fastest.
Arguments:
- coords: float32 [2, 24576], P(None, ('row', 'col')), may hold values from 0 to 1
- prior: float32 [24576, 16384], P(('row', 'col'), 'depth'), may hold values from -0.057409916 to 0.057409916, as said below
- target: float32 [1024], replicated, may hold values from -6 to 6
- carried: float32 [16384], P('depth'), may hold values from -6 to 6
- variance: float32 [1], replicated, may hold values from 1 to 2
- lengthscale: float32 [1], replicated, may hold values from 0.1 to 0.4
- nugget: float32 [1], replicated, may hold values from 14 to 16
Outputs:
- panels: float32 [24576, 1024], P(('row', 'col'))
- solved: float32 [1024], replicated
The draws below stay inside these ranges and needn't reach their ends.
Inputs may be any that keep to these rules, and one draw needn't show every extreme that they name: `prior`: independent entries of mean zero.
All inputs are finite; a program needn't handle non-finite values.
Results may differ from the reference program's by a relative error of at most 0.00011.
Values sent between devices are 32-bit elements; how exact they have to be, the bound alone decides.
A program may use at most 128 MiB of HBM per device.

```python
import math
import jax
import jax.numpy as jnp
from jax import lax

PANEL = 512
ROWS = 24576
PRIOR = 16384


def draw_prior(key, part):
    spread = math.sqrt(6.0 / PRIOR)
    value = jax.random.uniform(key, (ROWS, PRIOR), jnp.float32, -1.7320508, 1.7320508)
    return value * spread


def steps_of(stream_key, shape, shards, least, largest):
    factor_of, own = 1.0, jax.random.fold_in(stream_key, 6)
    for dim, shards_of in shards:
        heights = jnp.exp(jax.random.uniform(jax.random.fold_in(own, dim), (shards_of,), jnp.float32, least / len(shards), largest / len(shards)))
        factor_of = factor_of * jnp.repeat(heights, shape[dim] // shards_of).reshape([-1 if axis == dim else 1 for axis in range(len(shape))])
    return factor_of


def gaussian(key, shape, scale, reach, pieces=(), kind=jnp.bfloat16):
    values = scale * jax.random.normal(key, shape, jnp.float32)
    if pieces:
        values = values * steps_of(key, shape, pieces, -0.22, 0.18)
    return jnp.clip(values, -reach, reach).astype(kind)


def setup_inputs(seed: int = 0) -> dict:
    keys = jax.random.split(jax.random.key(seed), 8)
    coords = jnp.clip(1.0 * jax.random.uniform(keys[0], (2, ROWS), jnp.float32) ** steps_of(keys[0], (2, ROWS), ((1, 16),), -0.2, 0.2), 0.0, 1.0)
    prior = draw_prior(jax.random.fold_in(keys[7], 71), 0)
    target = gaussian(keys[2], (2 * PANEL,), 1.0, 6.0, (), jnp.float32)
    carried = gaussian(keys[3], (PRIOR,), 1.0, 6.0, ((0, 8),), jnp.float32)
    variance = jnp.clip(jax.random.uniform(keys[4], (1,), jnp.float32, 1.0, 2.0), 1.0, 2.0)
    lengthscale = jnp.clip(jnp.exp(jax.random.uniform(keys[5], (1,), jnp.float32, math.log(0.1), math.log(0.4))), 0.1, 0.4)
    nugget = jnp.clip(jax.random.uniform(keys[6], (1,), jnp.float32, 14.0, 16.0), 14.0, 16.0)
    return {"coords": coords, "prior": prior, "target": target, "carried": carried, "variance": variance, "lengthscale": lengthscale, "nugget": nugget}


root_three = 1.7320508075688772

def matern(left_xy, right_xy, variance, lengthscale):
    delta_x = left_xy[0][:, None] - right_xy[0][None, :]
    delta_y = left_xy[1][:, None] - right_xy[1][None, :]
    scaled = root_three * jnp.sqrt(delta_x * delta_x + delta_y * delta_y) / lengthscale[0]
    return variance[0] * (1.0 + scaled) * jnp.exp(-scaled)

def inverse_factor(block):
    lower = jnp.linalg.cholesky(block)
    ident = jnp.eye(block.shape[0], dtype=block.dtype)
    return lax.linalg.triangular_solve(lower, ident, left_side=True, lower=True)

def times_inverse(left, inverse):
    return jnp.einsum('rk,ck->rc', left, inverse, precision=lax.Precision.HIGHEST)

def reference(coords, prior, target, carried, variance, lengthscale, nugget):
    highest = lax.Precision.HIGHEST
    width = 2 * PANEL
    kernel = matern(coords, coords[:, :width], variance, lengthscale)
    diagonal = jnp.arange(ROWS, dtype=jnp.int32)[:, None] == jnp.arange(width, dtype=jnp.int32)[None, :]
    kernel = kernel + jnp.where(diagonal, nugget[0], 0.0)
    head = prior[:width]
    update = kernel - jnp.einsum('rk,ck->rc', prior, head, precision=highest)
    residual = target - jnp.dot(head, carried, precision=highest)
    inverse_one = inverse_factor(update[:PANEL, :PANEL])
    first = times_inverse(update[:, :PANEL], inverse_one)
    link = first[PANEL:width]
    rest = update[:, PANEL:] - jnp.einsum('rk,ck->rc', first, link, precision=highest)
    inverse_two = inverse_factor(rest[PANEL:width])
    second = times_inverse(rest, inverse_two)
    z_one = jnp.dot(inverse_one, residual[:PANEL], precision=highest)
    z_two = jnp.dot(inverse_two, residual[PANEL:] - jnp.dot(link, z_one, precision=highest), precision=highest)
    return (jnp.concatenate([first, second], axis=1), jnp.concatenate([z_one, z_two]))
```

```python
import functools

import jax
import jax.numpy as jnp
from jax import lax
from jax.experimental import pallas as pl
from jax.experimental.pallas import tpu as pltpu
from jax.sharding import PartitionSpec as P

f32 = jnp.float32
MESH = pl.DeviceIdType.MESH
B = 128
root_three = 1.7320508075688772


def split(x):
    hi = x.astype(jnp.bfloat16)
    return hi, (x - hi.astype(f32)).astype(jnp.bfloat16)


def iota8():
    shape = (8, B)
    return lax.broadcasted_iota(jnp.int32, shape, 0), lax.broadcasted_iota(jnp.int32, shape, 1)

def base(x, b=32):
    n=B; row8,col8=iota8()
    T=n//8; nt=b//8
    X=[x[8*t:8*t+8] for t in range(T)]
    out=[]
    for blk in range(n//b):
        c0=blk*b; t0=c0//8
        C=[[jnp.broadcast_to(X[t0+t][:,c0+k:c0+k+1],(8,n)) for k in range(8*t+8)] for t in range(nt)]
        inb=(col8>=c0)&(col8<c0+b)
        E=[jnp.where(inb,(col8==row8+(c0+8*t)).astype(f32),X[t0+t]) for t in range(nt)]
        scale=[None]*nt
        for j in range(b):
            tj,sj=divmod(j,8)
            p=C[tj][j][sj:sj+1,:]
            pinv=1.0/p
            rs=lax.rsqrt(p)
            scale[tj]=jnp.broadcast_to(rs,(8,n)) if sj==0 else jnp.where(row8==sj,rs,scale[tj])
            er=E[tj][sj:sj+1,:]*pinv
            rk={}
            for k in range(j+1,b):
                tk,sk=divmod(k,8)
                rk[k]=C[tk][j][sk:sk+1,:]*pinv
            for t in range(tj,nt):
                c=C[t][j]
                for k in range(j+1,8*t+8):
                    C[t][k]=C[t][k]-c*rk[k]
                ce=jnp.where(row8>sj,c,0.0) if t==tj else c
                if not (t==tj and sj==7):
                    E[t]=E[t]-ce*er
        U=[E[t]*scale[t] for t in range(nt)]
        out+=U
        if c0+b<n:
            u=jnp.concatenate(U,axis=0)
            at=u.T[c0+b:]
            ah,al=split(at); bh,bl=split(u)
            l=jnp.concatenate([ah,al,ah],axis=1); r=jnp.concatenate([bh,bh,bl],axis=0)
            d=jnp.dot(l,r,preferred_element_type=f32)
            for t in range(t0+nt,T):
                o=8*t-(c0+b)
                X[t]=jnp.where(inb,0.0,X[t])-d[o:o+8]
    w=jnp.concatenate(out,axis=0)
    rr=lax.broadcasted_iota(jnp.int32,(n,n),0); cc=lax.broadcasted_iota(jnp.int32,(n,n),1)
    return jnp.where(cc<=rr,w,0.0)


WAY_IN = {(0, 1): 0, (3, 0): 2, (0, 3): 0, (1, 0): 2, (0, 2): 0, (2, 0): 2, (1, 1): 2, (3, 1): 1, (3, 3): 3,
          (1, 3): 2, (1, 2): 2, (2, 1): 1, (3, 2): 3, (2, 3): 2, (2, 2): 1}
STEP = ((1, 0), (0, 1), (-1, 0), (0, -1))

def tree_kids():
    kids = [[[] for _ in range(4)] for _ in range(4)]
    for node, way in WAY_IN.items():
        for q in range(4):
            x, y = node
            for _ in range(q):
                x, y = (-y) % 4, x
            e = (way + q) % 4
            kids[q][e].append((x - STEP[e][0]) % 4 + 4 * ((y - STEP[e][1]) % 4))
    return kids
KIDS = tree_kids()

def tree_depths():
    out = [[0] * 16 for _ in range(4)]
    for node in WAY_IN:
        u, k = node, 0
        while u != (0, 0):
            s = STEP[WAY_IN[u]]
            u, k = ((u[0] - s[0]) % 4, (u[1] - s[1]) % 4), k + 1
        x, y = node
        for q in range(4):
            out[q][x + 4 * y] = k
            x, y = (-y) % 4, x
    return out
DEPTH = tree_depths()


def bkernel(R, D, prior_ref, out_ref, head, send_sem, recv_sem, osem):
    x, y = lax.axis_index("col"), lax.axis_index("row")
    z = lax.axis_index("depth")
    node = x + 4 * y
    nbr = [{"col": lax.rem(x + 4 + sx, 4), "row": lax.rem(y + 4 + sy, 4)} for sx, sy in STEP]
    sends = {}
    for q in range(4):
        for e in range(4):
            ks = KIDS[q][e]
            if ks:
                sends[q, e] = functools.reduce(jnp.logical_or, [node == k for k in ks])
    barrier = pltpu.get_barrier_semaphore()
    for e in range(4):
        pl.semaphore_signal(barrier, inc=1, device_id=nbr[e], device_id_type=MESH)
    pl.semaphore_wait(barrier, 4)
    C = 256 // R
    def rows(q, c):
        return pl.ds(pl.multiple_of((c * 4 + q) * R, R), R)
    def copy(q, e, c, src):
        return pltpu.make_async_remote_copy(src_ref=src.at[rows(q, c)], dst_ref=head.at[rows(q, c)],
            send_sem=send_sem.at[q, e], recv_sem=recv_sem.at[q, c], device_id=nbr[e], device_id_type=MESH)
    @pl.when(node == 0)
    def _():
        def body(c, _):
            for q in range(4):
                for e in range(4):
                    if (q, e) in sends and 0 in KIDS[q][e]:
                        copy(q, e, c, prior_ref).start()
            return 0
        lax.fori_loop(0, C, body, 0)
        cp = pltpu.make_async_copy(prior_ref.at[pl.ds(0, 1024)], head, osem)
        cp.start(); cp.wait()
    depth = [sum(jnp.where(node == v, D * DEPTH[q][v], 0) for v in range(1, 16)) for q in range(4)]
    deepest = max(max(d) for d in DEPTH)
    @pl.when(node != 0)
    def _():
        def body(s, _):
            for q in range(4):
                c = s + D - depth[q]
                @pl.when((c >= 0) & (c < C))
                def _():
                    copy(q, 0, c, head).wait_recv()
                    for e in range(4):
                        if (q, e) in sends and any(k != 0 for k in KIDS[q][e]):
                            @pl.when(sends[q, e])
                            def _():
                                copy(q, e, c, head).start()
            return 0
        lax.fori_loop(0, C + D * (deepest - 1), body, 0)
    for (q, e), has in sends.items():
        @pl.when(has)
        def _():
            pltpu.make_async_remote_copy(src_ref=head.at[pl.ds(0, 256)], dst_ref=head.at[pl.ds(0, 256)],
                send_sem=send_sem.at[q, e], recv_sem=recv_sem.at[0, 0], device_id=nbr[e], device_id_type=MESH).wait_send()
    cp = pltpu.make_async_copy(head, out_ref, osem)
    cp.start(); cp.wait()

def bcast(prior, R=16, D=1):
    return pl.pallas_call(
        functools.partial(bkernel, R, D),
        out_shape=jax.ShapeDtypeStruct((1024, 2048), f32),
        in_specs=[pl.BlockSpec(memory_space=pl.ANY)],
        out_specs=pl.BlockSpec(memory_space=pl.ANY),
        scratch_shapes=[pltpu.VMEM((1024, 2048), f32), pltpu.SemaphoreType.DMA((4, 4)), pltpu.SemaphoreType.DMA((4, 256 // R)), pltpu.SemaphoreType.DMA],
        compiler_params=pltpu.CompilerParams(collective_id=1, has_side_effects=True, vmem_limit_bytes=50 << 20),
    )(prior)


def sl(a):
    h, l = split(a); return jnp.concatenate([h, l, h], axis=1)
def sr(b):
    h, l = split(b); return jnp.concatenate([h, h, l], axis=0)
def mm(l, r):
    return jnp.dot(l, r, preferred_element_type=f32)

def chol_kernel(a_ref, w_ref, b_ref, m_ref):
    n = a_ref.shape[0]
    nb = n // B
    b_ref[...] = a_ref[...]
    ri = lax.broadcasted_iota(jnp.int32, (B, n), 0)
    ci = lax.broadcasted_iota(jnp.int32, (B, n), 1)
    m_ref[...] = base(b_ref[0:B, 0:B])
    def step(k, _):
        ks = pl.multiple_of(k * B, B)
        kn = pl.multiple_of(jnp.minimum(k + 1, nb - 1) * B, B)
        m = m_ref[...]
        inblk = (ci >= ks) & (ci < ks + B)
        row = jnp.where(inblk, (ci == ri + ks).astype(f32), b_ref[pl.ds(ks, B), :])
        r = mm(sl(m), sr(row))
        w_ref[pl.ds(ks, B), :] = jnp.where(ci < ks + B, r, 0.0)
        rs = sr(r)
        mt = sr(m.T)
        g = mm(sl(b_ref[pl.ds(kn, B), pl.ds(ks, B)]), mt)
        nxt = jnp.where(inblk, 0.0, b_ref[pl.ds(kn, B), :]) - mm(sl(g), rs)
        b_ref[pl.ds(kn, B), :] = nxt
        m_ref[...] = base(b_ref[pl.ds(kn, B), pl.ds(kn, B)])
        rows = lax.broadcasted_iota(jnp.int32, (n, 1), 0)
        act = rows >= ks + 2 * B
        g = jnp.where(act, mm(sl(b_ref[:, pl.ds(ks, B)]), mt), 0.0)
        gs = sl(g)
        for i in range(2, nb):
            z = (act[i * B:(i + 1) * B]) & inblk
            cur = jnp.where(z, 0.0, b_ref[i * B:(i + 1) * B, :])
            b_ref[i * B:(i + 1) * B, :] = cur - mm(gs[i * B:(i + 1) * B], rs)
        return 0
    lax.fori_loop(0, nb, step, 0)

def chol_inv(a):
    n = a.shape[0]
    return pl.pallas_call(
        chol_kernel,
        out_shape=jax.ShapeDtypeStruct((n, n), jnp.float32),
        in_specs=[pl.BlockSpec(memory_space=pltpu.VMEM)],
        out_specs=pl.BlockSpec(memory_space=pltpu.VMEM),
        scratch_shapes=[pltpu.VMEM((n, n), jnp.float32), pltpu.VMEM((B, B), jnp.float32)],
        compiler_params=pltpu.CompilerParams(vmem_limit_bytes=40 << 20),
    )(a)


def matern(left_xy, right_xy, variance, lengthscale):
    delta_x = left_xy[0][:, None] - right_xy[0][None, :]
    delta_y = left_xy[1][:, None] - right_xy[1][None, :]
    scaled = root_three * jnp.sqrt(delta_x * delta_x + delta_y * delta_y) / lengthscale[0]
    return variance[0] * (1.0 + scaled) * jnp.exp(-scaled)


def outer_rows(left, right):
    return jnp.einsum("rk,ck->rc", left, right, precision=lax.Precision.HIGH)


def local(coords, prior, target, carried, variance, lengthscale, nugget):
    highest = lax.Precision.HIGHEST
    width = 1024
    rows_dev = prior.shape[0]
    face = lax.axis_index(("row", "col"))
    head = bcast(prior, 8, 3)
    xy = jnp.where(face == 0, coords[:, :width], 0.0)
    head_xy = lax.psum(xy, ("row", "col"))
    gram = outer_rows(head, head)
    projected = jnp.dot(head, carried, precision=highest)
    gram, projected, summed = lax.psum((gram, projected, outer_rows(prior, head)), "depth")
    head_kernel = matern(head_xy, head_xy, variance, lengthscale) + nugget[0] * jnp.eye(width, dtype=f32)
    inverse = chol_inv(head_kernel - gram)
    solved = jnp.dot(inverse, target - projected, precision=highest)
    kernel = matern(coords, head_xy, variance, lengthscale)
    row_ids = face * rows_dev + jnp.arange(rows_dev, dtype=jnp.int32)
    col_ids = jnp.arange(width, dtype=jnp.int32)
    kernel = kernel + jnp.where(row_ids[:, None] == col_ids[None, :], nugget[0], 0.0)
    panels = outer_rows(kernel - summed, inverse)
    return (panels, solved)


def solution(mesh):
    return jax.shard_map(
        local,
        mesh=mesh,
        in_specs=(
            P(None, ("row", "col")),
            P(("row", "col"), "depth"),
            P(),
            P("depth"),
            P(),
            P(),
            P(),
        ),
        out_specs=(P(("row", "col"), None), P()),
        check_vma=False,
    )
```

```python
import functools

import jax
import jax.numpy as jnp
from jax import lax
from jax.experimental import pallas as pl
from jax.experimental.pallas import tpu as pltpu
from jax.sharding import PartitionSpec as P

f32 = jnp.float32
MESH = pl.DeviceIdType.MESH
B = 128
root_three = 1.7320508075688772


def split(x):
    hi = x.astype(jnp.bfloat16)
    return hi, (x - hi.astype(f32)).astype(jnp.bfloat16)


def iota8():
    shape = (8, B)
    return lax.broadcasted_iota(jnp.int32, shape, 0), lax.broadcasted_iota(jnp.int32, shape, 1)

def base(x, b=32):
    n=B; row8,col8=iota8()
    T=n//8; nt=b//8
    X=[x[8*t:8*t+8] for t in range(T)]
    out=[]
    for blk in range(n//b):
        c0=blk*b; t0=c0//8
        C=[[jnp.broadcast_to(X[t0+t][:,c0+k:c0+k+1],(8,n)) for k in range(8*t+8)] for t in range(nt)]
        inb=(col8>=c0)&(col8<c0+b)
        E=[jnp.where(inb,(col8==row8+(c0+8*t)).astype(f32),X[t0+t]) for t in range(nt)]
        scale=[None]*nt
        for j in range(b):
            tj,sj=divmod(j,8)
            p=C[tj][j][sj:sj+1,:]
            pinv=1.0/p
            rs=lax.rsqrt(p)
            scale[tj]=jnp.broadcast_to(rs,(8,n)) if sj==0 else jnp.where(row8==sj,rs,scale[tj])
            er=E[tj][sj:sj+1,:]*pinv
            rk={}
            for k in range(j+1,b):
                tk,sk=divmod(k,8)
                rk[k]=C[tk][j][sk:sk+1,:]*pinv
            for t in range(tj,nt):
                c=C[t][j]
                for k in range(j+1,8*t+8):
                    C[t][k]=C[t][k]-c*rk[k]
                ce=jnp.where(row8>sj,c,0.0) if t==tj else c
                if not (t==tj and sj==7):
                    E[t]=E[t]-ce*er
        U=[E[t]*scale[t] for t in range(nt)]
        out+=U
        if c0+b<n:
            u=jnp.concatenate(U,axis=0)
            at=u.T[c0+b:]
            ah,al=split(at); bh,bl=split(u)
            l=jnp.concatenate([ah,al,ah],axis=1); r=jnp.concatenate([bh,bh,bl],axis=0)
            d=jnp.dot(l,r,preferred_element_type=f32)
            for t in range(t0+nt,T):
                o=8*t-(c0+b)
                X[t]=jnp.where(inb,0.0,X[t])-d[o:o+8]
    w=jnp.concatenate(out,axis=0)
    rr=lax.broadcasted_iota(jnp.int32,(n,n),0); cc=lax.broadcasted_iota(jnp.int32,(n,n),1)
    return jnp.where(cc<=rr,w,0.0)


WAY_IN = {(0, 1): 0, (3, 0): 2, (0, 3): 0, (1, 0): 2, (0, 2): 0, (2, 0): 2, (1, 1): 2, (3, 1): 1, (3, 3): 3,
          (1, 3): 2, (1, 2): 2, (2, 1): 1, (3, 2): 3, (2, 3): 2, (2, 2): 1}
STEP = ((1, 0), (0, 1), (-1, 0), (0, -1))

def tree_kids():
    kids = [[[] for _ in range(4)] for _ in range(4)]
    for node, way in WAY_IN.items():
        for q in range(4):
            x, y = node
            for _ in range(q):
                x, y = (-y) % 4, x
            e = (way + q) % 4
            kids[q][e].append((x - STEP[e][0]) % 4 + 4 * ((y - STEP[e][1]) % 4))
    return kids
KIDS = tree_kids()

def tree_depths():
    out = [[0] * 16 for _ in range(4)]
    for node in WAY_IN:
        u, k = node, 0
        while u != (0, 0):
            s = STEP[WAY_IN[u]]
            u, k = ((u[0] - s[0]) % 4, (u[1] - s[1]) % 4), k + 1
        x, y = node
        for q in range(4):
            out[q][x + 4 * y] = k
            x, y = (-y) % 4, x
    return out
DEPTH = tree_depths()


R = 8
D = 3
CH = 256 // R
DEEP = 5
PIECE = 192


def sl(a):
    h, l = split(a)
    return jnp.concatenate([h, l, h], axis=1)


def sr(b):
    h, l = split(b)
    return jnp.concatenate([h, h, l], axis=0)


def mm(left, right):
    return jnp.dot(left, right, preferred_element_type=f32)


def nt(left, right):
    return lax.dot_general(left, right, (((1,), (1,)), ((), ())), preferred_element_type=f32)


def nt3(lh, ll, rh, rl):
    return nt(lh, rh) + (nt(ll, rh) + nt(lh, rl))


def kernel(prior, coords_t, coords, carried, target, scal, u_out, w_out,
           head, ph, plo, hh, hl, part, sib, zr, full, wbuf, stage, xyh, pj,
           head_send, head_recv, w_send, w_recv, ws_send, ws_recv, x_send, x_recv,
           j_send, j_recv, p_send, p_recv, st_sem, o_sem):
    x, y, d = lax.axis_index("col"), lax.axis_index("row"), lax.axis_index("depth")
    z, core = lax.div(d, 2), lax.rem(d, 2)
    node = x + 4 * y
    nbr = [{"col": lax.rem(x + 4 + sx, 4), "row": lax.rem(y + 4 + sy, 4)} for sx, sy in STEP]
    sibling = {"depth": 2 * z + 1 - core}
    is_root = node == 0

    def zpeer(k):
        return {"depth": 2 * lax.rem(z + k, 4) + core}

    def remote(src, dst, ss, rs, dev):
        return pltpu.make_async_remote_copy(
            src_ref=src, dst_ref=dst, send_sem=ss, recv_sem=rs, device_id=dev, device_id_type=MESH)

    sends = {}
    for q in range(4):
        for e in range(4):
            if KIDS[q][e]:
                sends[q, e] = functools.reduce(jnp.logical_or, [node == k for k in KIDS[q][e]])
    depth = [sum(jnp.where(node == v, DEPTH[q][v], 0) for v in range(1, 16)) for q in range(4)]

    barrier = pltpu.get_barrier_semaphore()
    for e in range(4):
        pl.semaphore_signal(barrier, inc=1, device_id=nbr[e], device_id_type=MESH)
    for k in range(1, 8):
        pl.semaphore_signal(barrier, inc=1, device_id={"depth": lax.rem(d + k, 8)}, device_id_type=MESH)
    pl.semaphore_wait(barrier, 11)

    def hrows(q, c):
        return pl.ds(pl.multiple_of((c * 4 + q) * R, R), R)

    def hcopy(q, e, c, src):
        return remote(src.at[hrows(q, c)], head.at[hrows(q, c)], head_send.at[q, e], head_recv.at[q, c], nbr[e])

    def wrows(q, k, cr):
        return pl.ds(pl.multiple_of(k * B + cr * 64 + q * 16, 16), 16)

    def wcopy(q, e, k):
        r = wrows(q, k, core)
        return remote(wbuf.at[r], wbuf.at[r], w_send.at[q, e], w_recv.at[q, k], nbr[e])

    def wsib(q, k, cr):
        r = wrows(q, k, cr)
        return remote(wbuf.at[r], wbuf.at[r], ws_send, ws_recv.at[q, k], sibling)

    def xcopy(e, i):
        ref = xyh if i == 0 else wbuf.at[pl.ds(1024, 8)]
        return remote(ref, ref, x_send.at[i, e], x_recv.at[i], nbr[e])

    def forward(q, start):
        for e in range(4):
            if (q, e) in sends and any(k != 0 for k in KIDS[q][e]):
                @pl.when(sends[q, e])
                def _():
                    start(e)

    def root_send(q, start):
        for e in range(4):
            if (q, e) in sends and 0 in KIDS[q][e]:
                start(e)

    def arrive(s):
        for q in range(4):
            c = s - D * (depth[q] - 1)

            @pl.when((c >= 0) & (c < CH))
            def _():
                hcopy(q, 0, c, head).wait_recv()
                forward(q, lambda e: hcopy(q, e, c, head).start())
            if q == 0:
                @pl.when(c == 1)
                def _():
                    xcopy(0, 0).wait_recv()
                    forward(0, lambda e: xcopy(e, 0).start())

    def w_round(k0, n):
        def body(t, _):
            for q in range(4):
                k = k0 + t - (depth[q] - 1)

                @pl.when((k >= k0) & (k < k0 + n))
                def _():
                    wcopy(q, 0, k).wait_recv()
                    forward(q, lambda e: wcopy(q, e, k).start())
                    wsib(q, k, core).start()
            return 0
        lax.fori_loop(0, n + DEEP - 1, body, 0)

    def load(i, slot):
        rows = pl.ds(pl.multiple_of(i * PIECE, PIECE), PIECE)
        return pltpu.make_async_copy(prior.at[rows], stage.at[slot], st_sem.at[slot])

    def take(i):
        slot = lax.rem(i, 2)
        load(i, slot).wait()
        for t in range(0, PIECE, 16):
            h, l = split(stage[slot, t:t + 16, :])
            rows = pl.ds(pl.multiple_of(i * PIECE + t, 16), 16)
            ph[rows, :] = h
            plo[rows, :] = l

        @pl.when(i + 2 < 8)
        def _():
            load(i + 2, slot).start()

    def spot(job):
        cols, rb, s, so, zo, j = job
        return pl.ds(cols[0], cols[1]), rb, s, so, zo, j

    def own(job, zz, cr):
        _, rb, s, _, _, _ = job
        return pl.ds(pl.multiple_of(rb + cr * 4 * s + zz * s, 16), s)

    def a_copy(job):
        cols, rb, s, so, zo, j = spot(job)
        return remote(part.at[pl.ds(pl.multiple_of(rb + (1 - core) * 4 * s, 16), 4 * s), cols],
                      sib.at[pl.ds(so, 4 * s), cols], j_send.at[j, 0], j_recv.at[j, 0], sibling)

    def b_copy(job, k):
        cols, rb, s, so, zo, j = spot(job)
        return remote(part.at[own(job, lax.rem(z + k, 4), core), cols],
                      zr.at[k - 1, pl.ds(zo, s), cols], j_send.at[j, k], j_recv.at[j, k], zpeer(k))

    def c_copy(job, k):
        cols, rb, s, so, zo, j = spot(job)
        o = own(job, z, core)
        return remote(full.at[o, cols], full.at[o, cols], j_send.at[j, 3 + k], j_recv.at[j, 3 + k],
                      zpeer(k) if k < 4 else sibling)

    def d_copy(job, k, cr):
        cols, rb, s, so, zo, j = spot(job)
        o = own(job, lax.rem(z + 4 - k, 4), cr)
        return remote(full.at[o, cols], full.at[o, cols], j_send.at[j, 7 + k], j_recv.at[j, 7 + k], sibling)

    def step_a(job):
        a_copy(job).start()

    def step_b(job):
        cols, rb, s, so, zo, j = spot(job)
        a_copy(job).wait_recv()

        def body(i, _):
            o = pl.ds(pl.multiple_of(rb + core * 4 * s + i * 32, 32), 32)
            part[o, cols] = part[o, cols] + sib[pl.ds(pl.multiple_of(so + i * 32, 32), 32), cols]
            return 0
        lax.fori_loop(0, s // 8, body, 0)
        for k in (2, 1, 3):
            b_copy(job, k).start()

    def step_c(job, nugget):
        cols, rb, s, so, zo, j = spot(job)
        wide = job[0][1]
        for k in (1, 2, 3):
            b_copy(job, k).wait_recv()
        hx, hy = xyh[0:1, cols], xyh[1:2, cols]

        def body(i, _):
            first = rb + core * 4 * s + z * s + i * 32
            o = pl.ds(pl.multiple_of(first, 32), 32)
            t = pl.ds(pl.multiple_of(zo + i * 32, 32), 32)
            total = part[o, cols] + zr[0, t, cols] + (zr[1, t, cols] + zr[2, t, cols])
            dx = coords_t[o, 0:1] - hx
            dy = coords_t[o, 1:2] - hy
            scaled = root_three * jnp.sqrt(dx * dx + dy * dy) / scal[1]
            val = scal[0] * (1.0 + scaled) * jnp.exp(-scaled)
            if nugget:
                ri = lax.broadcasted_iota(jnp.int32, (32, wide), 0) + first
                ci = lax.broadcasted_iota(jnp.int32, (32, wide), 1) + job[0][0]
                val = val + jnp.where(ri == ci, scal[2], 0.0)
            full[o, cols] = val - total
            return 0
        lax.fori_loop(0, s // 32, body, 0)
        for k in (2, 1, 3, 4):
            c_copy(job, k).start()

    def step_d(job):
        for k in (1, 3, 2):
            c_copy(job, k).wait_recv()
            d_copy(job, k, core).start()

    def step_e(job):
        c_copy(job, 4).wait_recv()
        for k in (1, 2, 3):
            d_copy(job, k, 1 - core).wait_recv()

    def job_done(job):
        a_copy(job).wait_send()
        for k in (1, 2, 3):
            b_copy(job, k).wait_send()
            c_copy(job, k).wait_send()
            d_copy(job, k, core).wait_send()
        c_copy(job, 4).wait_send()

    load(0, 0).start()
    load(1, 1).start()

    @pl.when(is_root)
    def _():
        xyh[0:2, :] = coords[:, 0:1024]

        def send(c, _):
            for q in range(4):
                root_send(q, lambda e: hcopy(q, e, c, prior).start())

            @pl.when(c == 1)
            def _():
                root_send(0, lambda e: xcopy(e, 0).start())
            return 0
        lax.fori_loop(0, CH, send, 0)

        def tk(i, _):
            take(i)
            return 0
        lax.fori_loop(0, 8, tk, 0)
        gram = [((256 * c, 256), 256 * c, 32 * (4 - c), 0, 0, c) for c in range(4)]
        rest = ((0, 1024), 1024, 64, 512, 128, 4)

        def blk(rb, c):
            r = pl.ds(pl.multiple_of(rb * 256, 256), 256)
            cc = pl.ds(pl.multiple_of(c * 256, 256), 256)
            part[r, cc] = nt3(ph[r, :], plo[r, :], ph[cc, :], plo[cc, :])
        for c in range(4):
            def body(rb, _):
                blk(rb, c)
                return 0
            lax.fori_loop(c, 4, body, 0)
            step_a(gram[c])
            if c:
                step_b(gram[c - 1])
        step_b(gram[3])
        ch, cl = split(jnp.broadcast_to(carried[...], (16, 2048)))

        def pbody(c, _):
            cc = pl.ds(pl.multiple_of(c * 256, 256), 256)
            pj[0, :, cc] = nt3(ch, cl, ph[cc, :], plo[cc, :])[0:8]
            return 0
        lax.fori_loop(0, 4, pbody, 0)

        def pcopy(k):
            return remote(pj.at[0], pj.at[k], p_send.at[k - 1], p_recv.at[k - 1], {"depth": lax.rem(d + k, 8)})
        for k in range(1, 8):
            pcopy(k).start()
        step_c(gram[0], True)
        step_c(gram[1], True)

        def rbody(i, _):
            blk(4 + lax.div(i, 4), lax.rem(i, 4))
            return 0
        lax.fori_loop(0, 8, rbody, 0)
        step_a(rest)
        step_d(gram[0])
        step_c(gram[2], True)
        n = 1024
        head[:, 0:n] = jnp.zeros((n, n), f32)

        def merge(c):
            step_e(gram[c])
            lo, hi = 256 * c, 256 * c + 256
            head[lo:n, lo:hi] = head[lo:n, lo:hi] + full[lo:n, lo:hi]
            if c < 3:
                t = full[hi:n, lo:hi].T
                head[lo:hi, hi:n] = head[lo:hi, hi:n] + t
                full[lo:hi, hi:n] = t
        merge(0)
        ri = lax.broadcasted_iota(jnp.int32, (B, n), 0)
        ci = lax.broadcasted_iota(jnp.int32, (B, n), 1)
        rows = lax.broadcasted_iota(jnp.int32, (n, 1), 0)

        def step(k, _):
            @pl.when(k == 1)
            def _():
                step_d(gram[1])
                step_c(gram[3], True)

            @pl.when(k == 2)
            def _():
                merge(1)
                step_d(gram[2])

            @pl.when(k == 3)
            def _():
                step_d(gram[3])
                step_b(rest)

            @pl.when(k == 4)
            def _():
                merge(2)

            @pl.when(k == 5)
            def _():
                step_c(rest, False)

            @pl.when(k == 6)
            def _():
                merge(3)

            @pl.when(k == 7)
            def _():
                step_d(rest)
            ks = pl.multiple_of(k * B, B)
            m = base(head[pl.ds(ks, B), pl.ds(ks, B)])
            inblk = (ci >= ks) & (ci < ks + B)
            row = jnp.where(inblk, (ci == ri + ks).astype(f32), head[pl.ds(ks, B), 0:n])
            r = mm(sl(m), sr(row))
            wbuf[pl.ds(ks, B), :] = jnp.where(ci < ks + B, r, 0.0)
            for q in range(4):
                root_send(q, lambda e: wcopy(q, e, k).start())
            rs = sr(r)
            mt = sr(m.T)
            act = rows >= ks + B
            gs = sl(jnp.where(act, mm(sl(head[:, pl.ds(ks, B)]), mt), 0.0))
            for i in range(1, 8):
                zap = act[i * B:(i + 1) * B] & inblk
                cur = jnp.where(zap, 0.0, head[i * B:(i + 1) * B, 0:n])
                head[i * B:(i + 1) * B, 0:n] = cur - mm(gs[i * B:(i + 1) * B], rs)
            return 0
        lax.fori_loop(0, 8, step, 0)
        for k in range(1, 8):
            pcopy(k).wait_recv()
        proj = functools.reduce(jnp.add, [pj[k] for k in range(8)])
        rh, rl = split(jnp.concatenate([target[...] - proj] * 2, axis=0))

        def sbody(i, _):
            cc = pl.ds(pl.multiple_of(i * 256, 256), 256)
            wh, wl = split(wbuf[cc, :])
            wbuf[1024:1032, cc] = nt3(rh, rl, wh, wl)[0:8]
            return 0
        lax.fori_loop(0, 4, sbody, 0)
        root_send(0, lambda e: xcopy(e, 1).start())
        step_e(rest)
        for job in gram + [rest]:
            job_done(job)
        for k in range(1, 8):
            pcopy(k).wait_send()

    @pl.when(jnp.logical_not(is_root))
    def _():
        jobs = [((256 * c, 256), 0, 192, 0, 0, c) for c in range(4)]

        def early(s, _):
            arrive(s)
            take(s)
            return 0
        lax.fori_loop(0, 8, early, 0)
        lead = 8 + D * (DEEP - 1)

        def wait_only(s, _):
            arrive(s)
            return 0
        lax.fori_loop(8, lead, wait_only, 0)

        def block(m, with_arrivals):
            for t in range(0, 256, 16):
                h, l = split(head[pl.ds(pl.multiple_of(m * 256 + t, 16), 16), :])
                hh[t:t + 16, :] = h
                hl[t:t + 16, :] = l

            def piece(i, _):
                if with_arrivals:
                    arrive(lead + 8 * m + i)
                r = pl.ds(pl.multiple_of(i * PIECE, PIECE), PIECE)
                part[r, pl.ds(pl.multiple_of(m * 256, 256), 256)] = nt3(ph[r, :], plo[r, :], hh[...], hl[...])
                return 0
            lax.fori_loop(0, 8, piece, 0)
        block(0, True)
        step_a(jobs[0])
        block(1, True)
        step_a(jobs[1])
        step_b(jobs[0])
        block(2, True)
        step_a(jobs[2])
        step_b(jobs[1])
        step_c(jobs[0], False)
        block(3, False)
        step_a(jobs[3])
        step_b(jobs[2])
        step_c(jobs[1], False)
        step_d(jobs[0])
        step_b(jobs[3])
        step_c(jobs[2], False)
        step_d(jobs[1])
        w_round(0, 4)
        step_c(jobs[3], False)
        step_d(jobs[2])
        w_round(4, 3)
        step_d(jobs[3])
        for c in range(4):
            step_e(jobs[c])
        w_round(7, 1)
        xcopy(0, 1).wait_recv()
        forward(0, lambda e: xcopy(e, 1).start())
        for q in range(4):
            for k in range(8):
                wsib(q, k, 1 - core).wait_recv()
        for job in jobs:
            job_done(job)
        whole = wbuf.at[pl.ds(0, 512)]
        remote(whole, whole, ws_send, ws_recv.at[0, 0], sibling).wait_send()

    ucp = pltpu.make_async_copy(full, u_out, o_sem.at[0])
    wcp = pltpu.make_async_copy(wbuf, w_out, o_sem.at[1])
    ucp.start()
    wcp.start()
    for (q, e), has in sends.items():
        @pl.when(has)
        def _():
            ref = head.at[pl.ds(0, 256)]
            remote(ref, ref, head_send.at[q, e], head_recv.at[0, 0], nbr[e]).wait_send()
            ref = wbuf.at[pl.ds(0, 128)]
            remote(ref, ref, w_send.at[q, e], w_recv.at[0, 0], nbr[e]).wait_send()
            if q == 0:
                xcopy(e, 0).wait_send()
                xcopy(e, 1).wait_send()
    ucp.wait()
    wcp.wait()


def gather_and_factor(prior, coords, carried, target, scal):
    vm = pl.BlockSpec(memory_space=pltpu.VMEM)
    dma = pltpu.SemaphoreType.DMA
    bf = jnp.bfloat16
    return pl.pallas_call(
        kernel,
        out_shape=(jax.ShapeDtypeStruct((1536, 1024), f32), jax.ShapeDtypeStruct((1032, 1024), f32)),
        in_specs=[pl.BlockSpec(memory_space=pl.ANY), vm, vm, vm, vm, pl.BlockSpec(memory_space=pltpu.SMEM)],
        out_specs=(pl.BlockSpec(memory_space=pl.ANY), pl.BlockSpec(memory_space=pl.ANY)),
        scratch_shapes=[
            pltpu.VMEM((1024, 2048), f32),
            pltpu.VMEM((1536, 2048), bf), pltpu.VMEM((1536, 2048), bf),
            pltpu.VMEM((256, 2048), bf), pltpu.VMEM((256, 2048), bf),
            pltpu.VMEM((1536, 1024), f32), pltpu.VMEM((768, 1024), f32), pltpu.VMEM((3, 192, 1024), f32),
            pltpu.VMEM((1536, 1024), f32), pltpu.VMEM((1032, 1024), f32), pltpu.VMEM((2, PIECE, 2048), f32),
            pltpu.VMEM((8, 1024), f32), pltpu.VMEM((8, 8, 1024), f32),
            dma((4, 4)), dma((4, CH)), dma((4, 4)), dma((4, 8)), dma, dma((4, 8)), dma((2, 4)), dma((2,)),
            dma((5, 11)), dma((5, 11)), dma((7,)), dma((7,)), dma((2,)), dma((2,)),
        ],
        compiler_params=pltpu.CompilerParams(collective_id=1, has_side_effects=True, vmem_limit_bytes=60 << 20),
    )(prior, coords.T, coords, carried[None, :], target[None, :], scal)


def local(coords, prior, target, carried, variance, lengthscale, nugget):
    scal = jnp.concatenate([variance, lengthscale, nugget])
    update, inverse = gather_and_factor(prior, coords, carried, target, scal)
    panels = jnp.einsum("rk,ck->rc", update, inverse[:1024], precision=lax.Precision.HIGH)
    return (panels, inverse[1024])


def solution(mesh):
    return jax.shard_map(
        local,
        mesh=mesh,
        in_specs=(
            P(None, ("row", "col")),
            P(("row", "col"), "depth"),
            P(),
            P("depth"),
            P(),
            P(),
            P(),
        ),
        out_specs=(P(("row", "col"), None), P()),
        check_vma=False,
    )
```

```python
import functools

import jax
import jax.numpy as jnp
from jax import lax
from jax.experimental import pallas as pl
from jax.experimental.pallas import tpu as pltpu
from jax.sharding import PartitionSpec as P

f32 = jnp.float32
MESH = pl.DeviceIdType.MESH
B = 128
root_three = 1.7320508075688772


def split(x):
    hi = x.astype(jnp.bfloat16)
    return hi, (x - hi.astype(f32)).astype(jnp.bfloat16)


def iota8():
    shape = (8, B)
    return lax.broadcasted_iota(jnp.int32, shape, 0), lax.broadcasted_iota(jnp.int32, shape, 1)

def base(x, b=32):
    n=B; row8,col8=iota8()
    T=n//8; nt=b//8
    X=[x[8*t:8*t+8] for t in range(T)]
    out=[]
    for blk in range(n//b):
        c0=blk*b; t0=c0//8
        C=[[jnp.broadcast_to(X[t0+t][:,c0+k:c0+k+1],(8,n)) for k in range(8*t+8)] for t in range(nt)]
        inb=(col8>=c0)&(col8<c0+b)
        E=[jnp.where(inb,(col8==row8+(c0+8*t)).astype(f32),X[t0+t]) for t in range(nt)]
        scale=[None]*nt
        for j in range(b):
            tj,sj=divmod(j,8)
            p=C[tj][j][sj:sj+1,:]
            pinv=1.0/p
            rs=lax.rsqrt(p)
            scale[tj]=jnp.broadcast_to(rs,(8,n)) if sj==0 else jnp.where(row8==sj,rs,scale[tj])
            er=E[tj][sj:sj+1,:]*pinv
            rk={}
            for k in range(j+1,b):
                tk,sk=divmod(k,8)
                rk[k]=C[tk][j][sk:sk+1,:]*pinv
            for t in range(tj,nt):
                c=C[t][j]
                for k in range(j+1,8*t+8):
                    C[t][k]=C[t][k]-c*rk[k]
                ce=jnp.where(row8>sj,c,0.0) if t==tj else c
                if not (t==tj and sj==7):
                    E[t]=E[t]-ce*er
        U=[E[t]*scale[t] for t in range(nt)]
        out+=U
        if c0+b<n:
            u=jnp.concatenate(U,axis=0)
            at=u.T[c0+b:]
            ah,al=split(at); bh,bl=split(u)
            l=jnp.concatenate([ah,al,ah],axis=1); r=jnp.concatenate([bh,bh,bl],axis=0)
            d=jnp.dot(l,r,preferred_element_type=f32)
            for t in range(t0+nt,T):
                o=8*t-(c0+b)
                X[t]=jnp.where(inb,0.0,X[t])-d[o:o+8]
    w=jnp.concatenate(out,axis=0)
    rr=lax.broadcasted_iota(jnp.int32,(n,n),0); cc=lax.broadcasted_iota(jnp.int32,(n,n),1)
    return jnp.where(cc<=rr,w,0.0)


WAY_IN = {(0, 1): 0, (3, 0): 2, (0, 3): 0, (1, 0): 2, (0, 2): 0, (2, 0): 2, (1, 1): 2, (3, 1): 1, (3, 3): 3,
          (1, 3): 2, (1, 2): 2, (2, 1): 1, (3, 2): 3, (2, 3): 2, (2, 2): 1}
STEP = ((1, 0), (0, 1), (-1, 0), (0, -1))

def tree_kids():
    kids = [[[] for _ in range(4)] for _ in range(4)]
    for node, way in WAY_IN.items():
        for q in range(4):
            x, y = node
            for _ in range(q):
                x, y = (-y) % 4, x
            e = (way + q) % 4
            kids[q][e].append((x - STEP[e][0]) % 4 + 4 * ((y - STEP[e][1]) % 4))
    return kids
KIDS = tree_kids()

def tree_depths():
    out = [[0] * 16 for _ in range(4)]
    for node in WAY_IN:
        u, k = node, 0
        while u != (0, 0):
            s = STEP[WAY_IN[u]]
            u, k = ((u[0] - s[0]) % 4, (u[1] - s[1]) % 4), k + 1
        x, y = node
        for q in range(4):
            out[q][x + 4 * y] = k
            x, y = (-y) % 4, x
    return out
DEPTH = tree_depths()


R = 8
D = 3
CH = 256 // R
DEEP = 5
PIECE = 192


def sl(a):
    h, l = split(a)
    return jnp.concatenate([h, l, h], axis=1)


def sr(b):
    h, l = split(b)
    return jnp.concatenate([h, h, l], axis=0)


def mm(left, right):
    return jnp.dot(left, right, preferred_element_type=f32)


def nt(left, right):
    return lax.dot_general(left, right, (((1,), (1,)), ((), ())), preferred_element_type=f32)


def nt3(lh, ll, rh, rl):
    return nt(lh, rh) + (nt(ll, rh) + nt(lh, rl))


def kernel(prior, coords, carried, target, variance, lengthscale, nugget_ref, u_out, w_out,
           coords_t, head, ph, plo, hh, hl, part, sib, zr, full, wbuf, stage, xyh, pj,
           head_send, head_recv, w_send, w_recv, ws_send, ws_recv, x_send, x_recv,
           j_send, j_recv, p_send, p_recv, st_sem, o_sem):
    x, y, d = lax.axis_index("col"), lax.axis_index("row"), lax.axis_index("depth")
    z, core = lax.div(d, 2), lax.rem(d, 2)
    node = x + 4 * y
    nbr = [{"col": lax.rem(x + 4 + sx, 4), "row": lax.rem(y + 4 + sy, 4)} for sx, sy in STEP]
    sibling = {"depth": 2 * z + 1 - core}
    is_root = node == 0

    def zpeer(k):
        return {"depth": 2 * lax.rem(z + k, 4) + core}

    def remote(src, dst, ss, rs, dev):
        return pltpu.make_async_remote_copy(
            src_ref=src, dst_ref=dst, send_sem=ss, recv_sem=rs, device_id=dev, device_id_type=MESH)

    sends = {}
    for q in range(4):
        for e in range(4):
            if KIDS[q][e]:
                sends[q, e] = functools.reduce(jnp.logical_or, [node == k for k in KIDS[q][e]])
    depth = [sum(jnp.where(node == v, DEPTH[q][v], 0) for v in range(1, 16)) for q in range(4)]

    barrier = pltpu.get_barrier_semaphore()
    for e in range(4):
        pl.semaphore_signal(barrier, inc=1, device_id=nbr[e], device_id_type=MESH)
    for k in range(1, 8):
        pl.semaphore_signal(barrier, inc=1, device_id={"depth": lax.rem(d + k, 8)}, device_id_type=MESH)
    pl.semaphore_wait(barrier, 11)

    def hrows(q, c):
        return pl.ds(pl.multiple_of((c * 4 + q) * R, R), R)

    def hcopy(q, e, c, src):
        return remote(src.at[hrows(q, c)], head.at[hrows(q, c)], head_send.at[q, e], head_recv.at[q, c], nbr[e])

    def wrows(q, k, cr):
        return pl.ds(pl.multiple_of(k * B + cr * 64 + q * 16, 16), 16)

    def wcopy(q, e, k):
        r = wrows(q, k, core)
        return remote(wbuf.at[r], wbuf.at[r], w_send.at[q, e], w_recv.at[q, k], nbr[e])

    def wsib(q, k, cr):
        r = wrows(q, k, cr)
        return remote(wbuf.at[r], wbuf.at[r], ws_send, ws_recv.at[q, k], sibling)

    def xcopy(e, i):
        ref = xyh if i == 0 else wbuf.at[pl.ds(1024, 8)]
        return remote(ref, ref, x_send.at[i, e], x_recv.at[i], nbr[e])

    def forward(q, start):
        for e in range(4):
            if (q, e) in sends and any(k != 0 for k in KIDS[q][e]):
                @pl.when(sends[q, e])
                def _():
                    start(e)

    def root_send(q, start):
        for e in range(4):
            if (q, e) in sends and 0 in KIDS[q][e]:
                start(e)

    def arrive(s):
        for q in range(4):
            c = s - D * (depth[q] - 1)

            @pl.when((c >= 0) & (c < CH))
            def _():
                hcopy(q, 0, c, head).wait_recv()
                forward(q, lambda e: hcopy(q, e, c, head).start())
            if q == 0:
                @pl.when(c == 1)
                def _():
                    xcopy(0, 0).wait_recv()
                    forward(0, lambda e: xcopy(e, 0).start())

    def w_hop(k0, n, t):
        for q in range(4):
            k = k0 + t - (depth[q] - 1)

            @pl.when((k >= k0) & (k < k0 + n))
            def _():
                wcopy(q, 0, k).wait_recv()
                forward(q, lambda e: wcopy(q, e, k).start())
                wsib(q, k, core).start()
            if k0 == 0 and q == 0:
                @pl.when(k == 1)
                def _():
                    xcopy(0, 1).wait_recv()
                    forward(0, lambda e: xcopy(e, 1).start())

    def w_hops(k0, n, lo, hi):
        def body(t, _):
            w_hop(k0, n, t)
            return 0
        lax.fori_loop(lo, hi, body, 0)

    def load(i, slot):
        rows = pl.ds(pl.multiple_of(i * PIECE, PIECE), PIECE)
        return pltpu.make_async_copy(prior.at[rows], stage.at[slot], st_sem.at[slot])

    def take(i):
        slot = lax.rem(i, 2)
        load(i, slot).wait()
        for t in range(0, PIECE, 16):
            h, l = split(stage[slot, t:t + 16, :])
            rows = pl.ds(pl.multiple_of(i * PIECE + t, 16), 16)
            ph[rows, :] = h
            plo[rows, :] = l

        @pl.when(i + 2 < 8)
        def _():
            load(i + 2, slot).start()

    def spot(job):
        cols, rb, s, so, zo, j = job
        return pl.ds(cols[0], cols[1]), rb, s, so, zo, j

    def own(job, zz, cr):
        _, rb, s, _, _, _ = job
        return pl.ds(pl.multiple_of(rb + cr * 4 * s + zz * s, 16), s)

    def a_copy(job):
        cols, rb, s, so, zo, j = spot(job)
        return remote(part.at[pl.ds(pl.multiple_of(rb + (1 - core) * 4 * s, 16), 4 * s), cols],
                      sib.at[pl.ds(so, 4 * s), cols], j_send.at[j, 0], j_recv.at[j, 0], sibling)

    def b_copy(job, k):
        cols, rb, s, so, zo, j = spot(job)
        return remote(part.at[own(job, lax.rem(z + k, 4), core), cols],
                      zr.at[k - 1, pl.ds(zo, s), cols], j_send.at[j, k], j_recv.at[j, k], zpeer(k))

    def c_copy(job, k):
        cols, rb, s, so, zo, j = spot(job)
        o = own(job, z, core)
        return remote(full.at[o, cols], full.at[o, cols], j_send.at[j, 3 + k], j_recv.at[j, 3 + k],
                      zpeer(k) if k < 4 else sibling)

    def d_copy(job, k, cr):
        cols, rb, s, so, zo, j = spot(job)
        o = own(job, lax.rem(z + 4 - k, 4), cr)
        return remote(full.at[o, cols], full.at[o, cols], j_send.at[j, 7 + k], j_recv.at[j, 7 + k], sibling)

    def h_copy(job, half, zz, cr, dev, idx):
        cols, rb, s, so, zo, j = spot(job)
        o = pl.ds(pl.multiple_of(rb + cr * 4 * s + zz * s + half * (s // 2), 8), s // 2)
        return remote(full.at[o, cols], full.at[o, cols], j_send.at[j, idx], j_recv.at[j, idx], dev)

    def across(job, half):
        zz = lax.rem(z + (3 if half == 0 else 1), 4)
        return h_copy(job, half, zz, core, zpeer(1 if half == 0 else 3), 11 + half)

    def beside(job, half):
        return h_copy(job, half, lax.rem(z + 2, 4), core, sibling, 13 + half)

    def step_a(job):
        a_copy(job).start()

    def step_b(job):
        cols, rb, s, so, zo, j = spot(job)
        a_copy(job).wait_recv()

        def body(i, _):
            o = pl.ds(pl.multiple_of(rb + core * 4 * s + i * 32, 32), 32)
            part[o, cols] = part[o, cols] + sib[pl.ds(pl.multiple_of(so + i * 32, 32), 32), cols]
            return 0
        lax.fori_loop(0, s // 8, body, 0)
        for k in (2, 1, 3):
            b_copy(job, k).start()

    def step_c(job, nugget, relay=False):
        cols, rb, s, so, zo, j = spot(job)
        wide = job[0][1]
        for k in (1, 2, 3):
            b_copy(job, k).wait_recv()
        hx, hy = xyh[0:1, cols], xyh[1:2, cols]

        def body(i, _):
            first = rb + core * 4 * s + z * s + i * 32
            o = pl.ds(pl.multiple_of(first, 32), 32)
            t = pl.ds(pl.multiple_of(zo + i * 32, 32), 32)
            total = part[o, cols] + zr[0, t, cols] + (zr[1, t, cols] + zr[2, t, cols])
            dx = coords_t[o, 0:1] - hx
            dy = coords_t[o, 1:2] - hy
            scaled = root_three * jnp.sqrt(dx * dx + dy * dy) / lengthscale[0]
            val = variance[0] * (1.0 + scaled) * jnp.exp(-scaled)
            if nugget:
                ri = lax.broadcasted_iota(jnp.int32, (32, wide), 0) + first
                ci = lax.broadcasted_iota(jnp.int32, (32, wide), 1) + job[0][0]
                val = val + jnp.where(ri == ci, nugget_ref[0], 0.0)
            full[o, cols] = val - total
            return 0
        lax.fori_loop(0, s // 32, body, 0)
        for k in (1, 3, 4) if relay else (2, 1, 3, 4):
            c_copy(job, k).start()

    def step_d(job, relay=False):
        for k in (1, 3) if relay else (1, 3, 2):
            c_copy(job, k).wait_recv()
            if relay:
                across(job, 0 if k == 1 else 1).start()
            d_copy(job, k, core).start()

    def step_f(job):
        for half in (0, 1):
            across(job, half).wait_recv()
            beside(job, half).start()

    def step_e(job, relay=False):
        c_copy(job, 4).wait_recv()
        for k in (1, 3) if relay else (1, 2, 3):
            d_copy(job, k, 1 - core).wait_recv()
        if relay:
            for half in (0, 1):
                beside(job, half).wait_recv()

    def job_done(job, relay=False):
        a_copy(job).wait_send()
        for k in (1, 2, 3):
            b_copy(job, k).wait_send()
            if k != 2 or not relay:
                c_copy(job, k).wait_send()
                d_copy(job, k, core).wait_send()
        c_copy(job, 4).wait_send()
        if relay:
            for half in (0, 1):
                across(job, half).wait_send()
                beside(job, half).wait_send()

    load(0, 0).start()
    load(1, 1).start()
    coords_t[...] = jnp.concatenate([coords[...]] * 4, axis=0).T

    @pl.when(is_root)
    def _():
        xyh[0:2, :] = coords[:, 0:1024]

        def send(c, _):
            for q in range(4):
                root_send(q, lambda e: hcopy(q, e, c, prior).start())

            @pl.when(c == 1)
            def _():
                root_send(0, lambda e: xcopy(e, 0).start())
            return 0
        lax.fori_loop(0, CH, send, 0)

        def tk(i, _):
            take(i)
            return 0
        lax.fori_loop(0, 8, tk, 0)
        gram = [((256 * c, 256), 256 * c, 32 * (4 - c), 0, 0, c) for c in range(4)]
        rest = ((0, 1024), 1024, 64, 512, 128, 4)

        def blk(rb, n, c):
            cc = pl.ds(pl.multiple_of(c * 256, 256), 256)
            part[rb:rb + n, cc] = nt3(ph[rb:rb + n, :], plo[rb:rb + n, :], ph[cc, :], plo[cc, :])
        for c in range(4):
            blk(256 * c, 1024 - 256 * c, c)
            step_a(gram[c])
            if c:
                step_b(gram[c - 1])
        step_b(gram[3])
        step_c(gram[0], True)
        ch, cl = split(jnp.broadcast_to(carried[...], (16, 2048)))

        def pbody(c, _):
            cc = pl.ds(pl.multiple_of(c * 256, 256), 256)
            pj[0, :, cc] = nt3(ch, cl, ph[cc, :], plo[cc, :])[0:8]
            return 0
        lax.fori_loop(0, 4, pbody, 0)

        def pcopy(k):
            return remote(pj.at[0], pj.at[k], p_send.at[k - 1], p_recv.at[k - 1], {"depth": lax.rem(d + k, 8)})
        for k in range(1, 8):
            pcopy(k).start()
        step_c(gram[1], True)

        def rbody(i, _):
            r = pl.ds(pl.multiple_of(1024 + lax.div(i, 4) * 256, 256), 256)
            cc = pl.ds(pl.multiple_of(lax.rem(i, 4) * 256, 256), 256)
            part[r, cc] = nt3(ph[r, :], plo[r, :], ph[cc, :], plo[cc, :])
            return 0
        lax.fori_loop(0, 4, rbody, 0)
        step_d(gram[0])
        lax.fori_loop(4, 8, rbody, 0)
        step_a(rest)
        step_c(gram[2], True)
        n = 1024
        head[:, 0:n] = jnp.zeros((n, n), f32)

        def merge(c):
            step_e(gram[c])
            lo, hi = 256 * c, 256 * c + 256
            head[lo:n, lo:hi] = head[lo:n, lo:hi] + full[lo:n, lo:hi]
            if c < 3:
                t = full[hi:n, lo:hi].T
                head[lo:hi, hi:n] = head[lo:hi, hi:n] + t
                full[lo:hi, hi:n] = t
        merge(0)
        ri = lax.broadcasted_iota(jnp.int32, (B, n), 0)
        ci = lax.broadcasted_iota(jnp.int32, (B, n), 1)
        rows = lax.broadcasted_iota(jnp.int32, (n, 1), 0)

        def step(k, _):
            @pl.when(k == 1)
            def _():
                step_d(gram[1])
                step_c(gram[3], True)

            @pl.when(k == 2)
            def _():
                merge(1)
                step_d(gram[2])

            @pl.when(k == 3)
            def _():
                step_d(gram[3])
                step_b(rest)
                for i in range(1, 8):
                    pcopy(i).wait_recv()
                proj = functools.reduce(jnp.add, [pj[i] for i in range(8)])
                wbuf[1024:1032, :] = target[...] - proj
                root_send(0, lambda e: xcopy(e, 1).start())

            @pl.when(k == 4)
            def _():
                merge(2)

            @pl.when(k == 5)
            def _():
                step_c(rest, False)

            @pl.when(k == 6)
            def _():
                merge(3)

            @pl.when(k == 7)
            def _():
                step_d(rest)
            ks = pl.multiple_of(k * B, B)
            m = base(head[pl.ds(ks, B), pl.ds(ks, B)])
            inblk = (ci >= ks) & (ci < ks + B)
            row = jnp.where(inblk, (ci == ri + ks).astype(f32), head[pl.ds(ks, B), 0:n])
            r = mm(sl(m), sr(row))
            wbuf[pl.ds(ks, B), :] = jnp.where(ci < ks + B, r, 0.0)
            for q in range(4):
                root_send(q, lambda e: wcopy(q, e, k).start())

            @pl.when(k < 7)
            def _():
                rs = sr(r)
                mt = sr(m.T)
                act = rows >= ks + B
                gs = sl(jnp.where(act, mm(sl(head[:, pl.ds(ks, B)]), mt), 0.0))
                for i in range(1, 8):
                    zap = act[i * B:(i + 1) * B] & inblk
                    cur = jnp.where(zap, 0.0, head[i * B:(i + 1) * B, 0:n])
                    head[i * B:(i + 1) * B, 0:n] = cur - mm(gs[i * B:(i + 1) * B], rs)
            return 0
        lax.fori_loop(0, 8, step, 0)

        step_e(rest)
        for job in gram + [rest]:
            job_done(job)
        for k in range(1, 8):
            pcopy(k).wait_send()

    @pl.when(jnp.logical_not(is_root))
    def _():
        jobs = [((128 * c, 128), 0, 192, 0, 0, c) for c in range(8)]

        def early(s, _):
            arrive(s)
            take(s)
            return 0
        lax.fori_loop(0, 8, early, 0)
        lead = 4 + D * (DEEP - 1)

        def wait_only(s, _):
            arrive(s)
            return 0
        lax.fori_loop(8, lead, wait_only, 0)

        def block(m, hops=None):
            def cut(t, _):
                h, l = split(head[pl.ds(pl.multiple_of(m * 128 + t * 16, 16), 16), :])
                o = pl.ds(pl.multiple_of(t * 16, 16), 16)
                hh[o, :] = h
                hl[o, :] = l
                return 0
            lax.fori_loop(0, 8, cut, 0)

            def piece(i, _):
                if m < 7:
                    arrive(lead + 4 * m + i)
                r = pl.ds(pl.multiple_of(i * 384, 384), 384)
                part[r, m * 128:m * 128 + 128] = nt3(ph[r, :], plo[r, :], hh[...], hl[...])
                if hops is not None:
                    @pl.when(lax.rem(i, 2) == 1)
                    def _():
                        w_hop(0, 4, hops + lax.div(i, 2))
                return 0
            lax.fori_loop(0, 4, piece, 0)

        def tick(t):
            if t < 8:
                step_a(jobs[t])
            if 0 <= t - 1 < 8:
                step_b(jobs[t - 1])
            if 0 <= t - 2 < 8:
                step_c(jobs[t - 2], False, True)
            if 0 <= t - 3 < 8:
                step_d(jobs[t - 3], True)
            if 0 <= t - 4 < 8:
                step_f(jobs[t - 4])
        for m in range(8):
            block(m, 2 * (m - 5) if m >= 5 else None)
            tick(m)
        w_hops(0, 4, 6, 8)
        tick(8)
        w_hops(4, 4, 0, 3)
        tick(9)
        w_hops(4, 4, 3, 5)
        tick(10)
        w_hops(4, 4, 5, 7)
        tick(11)
        w_hops(4, 4, 7, 8)
        for c in range(8):
            step_e(jobs[c], True)
        for q in range(4):
            for k in range(8):
                wsib(q, k, 1 - core).wait_recv()
        for job in jobs:
            job_done(job, True)
        whole = wbuf.at[pl.ds(0, 512)]
        remote(whole, whole, ws_send, ws_recv.at[0, 0], sibling).wait_send()

    ucp = pltpu.make_async_copy(full, u_out, o_sem.at[0])
    wcp = pltpu.make_async_copy(wbuf, w_out, o_sem.at[1])
    ucp.start()
    wcp.start()
    for (q, e), has in sends.items():
        @pl.when(has)
        def _():
            ref = head.at[pl.ds(0, 256)]
            remote(ref, ref, head_send.at[q, e], head_recv.at[0, 0], nbr[e]).wait_send()
            ref = wbuf.at[pl.ds(0, 128)]
            remote(ref, ref, w_send.at[q, e], w_recv.at[0, 0], nbr[e]).wait_send()
            if q == 0:
                xcopy(e, 0).wait_send()
                xcopy(e, 1).wait_send()
    ucp.wait()
    wcp.wait()


def gather_and_factor(prior, coords, carried, target, scalars):
    vm = pl.BlockSpec(memory_space=pltpu.VMEM)
    sm = pl.BlockSpec(memory_space=pltpu.SMEM)
    dma = pltpu.SemaphoreType.DMA
    bf = jnp.bfloat16
    return pl.pallas_call(
        kernel,
        out_shape=(jax.ShapeDtypeStruct((1536, 1024), f32), jax.ShapeDtypeStruct((1032, 1024), f32)),
        in_specs=[pl.BlockSpec(memory_space=pl.ANY), vm, vm, vm, sm, sm, sm],
        out_specs=(pl.BlockSpec(memory_space=pl.ANY), pl.BlockSpec(memory_space=pl.ANY)),
        scratch_shapes=[
            pltpu.VMEM((1536, 8), f32),
            pltpu.VMEM((1024, 2048), f32),
            pltpu.VMEM((1536, 2048), bf), pltpu.VMEM((1536, 2048), bf),
            pltpu.VMEM((128, 2048), bf), pltpu.VMEM((128, 2048), bf),
            pltpu.VMEM((1536, 1024), f32), pltpu.VMEM((768, 1024), f32), pltpu.VMEM((3, 192, 1024), f32),
            pltpu.VMEM((1536, 1024), f32), pltpu.VMEM((1032, 1024), f32), pltpu.VMEM((2, PIECE, 2048), f32),
            pltpu.VMEM((8, 1024), f32), pltpu.VMEM((8, 8, 1024), f32),
            dma((4, 4)), dma((4, CH)), dma((4, 4)), dma((4, 8)), dma, dma((4, 8)), dma((2, 4)), dma((2,)),
            dma((8, 15)), dma((8, 15)), dma((7,)), dma((7,)), dma((2,)), dma((2,)),
        ],
        compiler_params=pltpu.CompilerParams(collective_id=1, has_side_effects=True, vmem_limit_bytes=60 << 20),
    )(prior, coords, carried[None, :], target[None, :], *scalars)


def panel_kernel(u, w, out, sol, wh, wl):
    @pl.when(pl.program_id(0) == 0)
    def _():
        def cut(t, _):
            o = pl.ds(pl.multiple_of(t * 16, 16), 16)
            h, l = split(w[o, :])
            wh[o, :] = h
            wl[o, :] = l
            return 0
        lax.fori_loop(0, 64, cut, 0)
        rh, rl = split(jnp.concatenate([w[1024:1032, :]] * 2, axis=0))
        for j in range(4):
            o = slice(256 * j, 256 * j + 256)
            sol[:, o] = nt3(rh, rl, wh[o, :], wl[o, :])[0:1]
    uh, ul = split(u[...])
    for j in range(4):
        o, n = slice(256 * j, 256 * j + 256), 256 * j + 256
        out[:, o] = nt3(uh[:, :n], ul[:, :n], wh[o, :n], wl[o, :n])


def panel_product(update, inverse):
    m = 384
    return pl.pallas_call(
        panel_kernel,
        grid=(1536 // m,),
        out_shape=(jax.ShapeDtypeStruct((1536, 1024), f32), jax.ShapeDtypeStruct((1, 1024), f32)),
        in_specs=[pl.BlockSpec((m, 1024), lambda i: (i, 0)), pl.BlockSpec((1032, 1024), lambda i: (0, 0))],
        out_specs=(pl.BlockSpec((m, 1024), lambda i: (i, 0)), pl.BlockSpec((1, 1024), lambda i: (0, 0))),
        scratch_shapes=[pltpu.VMEM((1024, 1024), jnp.bfloat16)] * 2,
        compiler_params=pltpu.CompilerParams(vmem_limit_bytes=48 << 20),
    )(update, inverse)


def local(coords, prior, target, carried, variance, lengthscale, nugget):
    update, inverse = gather_and_factor(prior, coords, carried, target, (variance, lengthscale, nugget))
    panels, solved = panel_product(update, inverse)
    return (panels, solved.reshape(1024))


def solution(mesh):
    return jax.shard_map(
        local,
        mesh=mesh,
        in_specs=(
            P(None, ("row", "col")),
            P(("row", "col"), "depth"),
            P(),
            P("depth"),
            P(),
            P(),
            P(),
        ),
        out_specs=(P(("row", "col"), None), P()),
        check_vma=False,
    )
```

```python
import functools

import jax
import jax.numpy as jnp
from jax import lax
from jax.experimental import pallas as pl
from jax.experimental.pallas import tpu as pltpu
from jax.sharding import PartitionSpec as P

f32 = jnp.float32
MESH = pl.DeviceIdType.MESH
B = 128
root_three = 1.7320508075688772


def split(x):
    hi = x.astype(jnp.bfloat16)
    return hi, (x - hi.astype(f32)).astype(jnp.bfloat16)


def iota8():
    shape = (8, B)
    return lax.broadcasted_iota(jnp.int32, shape, 0), lax.broadcasted_iota(jnp.int32, shape, 1)

def base(x, b=32):
    n=B; row8,col8=iota8()
    T=n//8; nt=b//8
    X=[x[8*t:8*t+8] for t in range(T)]
    out=[]
    for blk in range(n//b):
        c0=blk*b; t0=c0//8
        C=[[jnp.broadcast_to(X[t0+t][:,c0+k:c0+k+1],(8,n)) for k in range(8*t+8)] for t in range(nt)]
        inb=(col8>=c0)&(col8<c0+b)
        E=[jnp.where(inb,(col8==row8+(c0+8*t)).astype(f32),X[t0+t]) for t in range(nt)]
        scale=[None]*nt
        for j in range(b):
            tj,sj=divmod(j,8)
            p=C[tj][j][sj:sj+1,:]
            pinv=1.0/p
            rs=lax.rsqrt(p)
            scale[tj]=jnp.broadcast_to(rs,(8,n)) if sj==0 else jnp.where(row8==sj,rs,scale[tj])
            er=E[tj][sj:sj+1,:]*pinv
            rk={}
            for k in range(j+1,b):
                tk,sk=divmod(k,8)
                rk[k]=C[tk][j][sk:sk+1,:]*pinv
            for t in range(tj,nt):
                c=C[t][j]
                for k in range(j+1,8*t+8):
                    C[t][k]=C[t][k]-c*rk[k]
                ce=jnp.where(row8>sj,c,0.0) if t==tj else c
                if not (t==tj and sj==7):
                    E[t]=E[t]-ce*er
        U=[E[t]*scale[t] for t in range(nt)]
        out+=U
        if c0+b<n:
            u=jnp.concatenate(U,axis=0)
            at=u.T[c0+b:]
            ah,al=split(at); bh,bl=split(u)
            l=jnp.concatenate([ah,al,ah],axis=1); r=jnp.concatenate([bh,bh,bl],axis=0)
            d=jnp.dot(l,r,preferred_element_type=f32)
            for t in range(t0+nt,T):
                o=8*t-(c0+b)
                X[t]=jnp.where(inb,0.0,X[t])-d[o:o+8]
    w=jnp.concatenate(out,axis=0)
    rr=lax.broadcasted_iota(jnp.int32,(n,n),0); cc=lax.broadcasted_iota(jnp.int32,(n,n),1)
    return jnp.where(cc<=rr,w,0.0)


WAY_IN = {(0, 1): 0, (3, 0): 2, (0, 3): 0, (1, 0): 2, (0, 2): 0, (2, 0): 2, (1, 1): 2, (3, 1): 1, (3, 3): 3,
          (1, 3): 2, (1, 2): 2, (2, 1): 1, (3, 2): 3, (2, 3): 2, (2, 2): 1}
STEP = ((1, 0), (0, 1), (-1, 0), (0, -1))

def tree_kids():
    kids = [[[] for _ in range(4)] for _ in range(4)]
    for node, way in WAY_IN.items():
        for q in range(4):
            x, y = node
            for _ in range(q):
                x, y = (-y) % 4, x
            e = (way + q) % 4
            kids[q][e].append((x - STEP[e][0]) % 4 + 4 * ((y - STEP[e][1]) % 4))
    return kids
KIDS = tree_kids()

def tree_depths():
    out = [[0] * 16 for _ in range(4)]
    for node in WAY_IN:
        u, k = node, 0
        while u != (0, 0):
            s = STEP[WAY_IN[u]]
            u, k = ((u[0] - s[0]) % 4, (u[1] - s[1]) % 4), k + 1
        x, y = node
        for q in range(4):
            out[q][x + 4 * y] = k
            x, y = (-y) % 4, x
    return out
DEPTH = tree_depths()


R = 8
D = 3
CH = 256 // R
DEEP = 5
PIECE = 96


def sl(a):
    h, l = split(a)
    return jnp.concatenate([h, l, h], axis=1)


def sr(b):
    h, l = split(b)
    return jnp.concatenate([h, h, l], axis=0)


def mm(left, right):
    return jnp.dot(left, right, preferred_element_type=f32)


def nt(left, right):
    return lax.dot_general(left, right, (((1,), (1,)), ((), ())), preferred_element_type=f32)


def nt3(lh, ll, rh, rl):
    return nt(lh, rh) + (nt(ll, rh) + nt(lh, rl))


def kernel(prior, coords, carried, target, variance, lengthscale, nugget_ref, u_out, w_out,
           coords_t, head, ph, plo, hb, part, sib, zr, full, wbuf, stage, xyh, pj,
           head_send, head_recv, w_send, w_recv, ws_send, ws_recv, x_send, x_recv,
           j_send, j_recv, p_send, p_recv, st_sem, o_sem):
    x, y, d = lax.axis_index("col"), lax.axis_index("row"), lax.axis_index("depth")
    z, core = lax.div(d, 2), lax.rem(d, 2)
    node = x + 4 * y
    nbr = [{"col": lax.rem(x + 4 + sx, 4), "row": lax.rem(y + 4 + sy, 4)} for sx, sy in STEP]
    sibling = {"depth": 2 * z + 1 - core}
    is_root = node == 0

    def zpeer(k):
        return {"depth": 2 * lax.rem(z + k, 4) + core}

    def remote(src, dst, ss, rs, dev):
        return pltpu.make_async_remote_copy(
            src_ref=src, dst_ref=dst, send_sem=ss, recv_sem=rs, device_id=dev, device_id_type=MESH)

    sends = {}
    for q in range(4):
        for e in range(4):
            if KIDS[q][e]:
                sends[q, e] = functools.reduce(jnp.logical_or, [node == k for k in KIDS[q][e]])
    depth = [sum(jnp.where(node == v, DEPTH[q][v], 0) for v in range(1, 16)) for q in range(4)]

    barrier = pltpu.get_barrier_semaphore()
    for e in range(4):
        pl.semaphore_signal(barrier, inc=1, device_id=nbr[e], device_id_type=MESH)
    for k in range(1, 8):
        pl.semaphore_signal(barrier, inc=1, device_id={"depth": lax.rem(d + k, 8)}, device_id_type=MESH)
    pl.semaphore_wait(barrier, 11)

    def hrows(q, c):
        return pl.ds(pl.multiple_of((c * 4 + q) * R, R), R)

    def hcopy(q, e, c, src):
        return remote(src.at[hrows(q, c)], head.at[hrows(q, c)], head_send.at[q, e], head_recv.at[q, c], nbr[e])

    def wrows(q, k, cr):
        return pl.ds(pl.multiple_of(k * B + cr * 64 + q * 16, 16), 16)

    def wcopy(q, e, k):
        r = wrows(q, k, core)
        return remote(wbuf.at[r], wbuf.at[r], w_send.at[q, e], w_recv.at[q, k], nbr[e])

    def wsib(q, k, cr):
        r = wrows(q, k, cr)
        return remote(wbuf.at[r], wbuf.at[r], ws_send, ws_recv.at[q, k], sibling)

    def xcopy(e, i):
        ref = xyh if i == 0 else wbuf.at[pl.ds(1024, 8)]
        return remote(ref, ref, x_send.at[i, e], x_recv.at[i], nbr[e])

    def forward(q, start):
        for e in range(4):
            if (q, e) in sends and any(k != 0 for k in KIDS[q][e]):
                @pl.when(sends[q, e])
                def _():
                    start(e)

    def root_send(q, start):
        for e in range(4):
            if (q, e) in sends and 0 in KIDS[q][e]:
                start(e)

    def arrive(s):
        for q in range(4):
            c = s - D * (depth[q] - 1)

            @pl.when((c >= 0) & (c < CH))
            def _():
                hcopy(q, 0, c, head).wait_recv()
                forward(q, lambda e: hcopy(q, e, c, head).start())
            if q == 0:
                @pl.when(c == 1)
                def _():
                    xcopy(0, 0).wait_recv()
                    forward(0, lambda e: xcopy(e, 0).start())

    def w_hop(k0, n, t):
        for q in range(4):
            k = k0 + t - (depth[q] - 1)

            @pl.when((k >= k0) & (k < k0 + n))
            def _():
                wcopy(q, 0, k).wait_recv()
                forward(q, lambda e: wcopy(q, e, k).start())
                wsib(q, k, core).start()
            if k0 == 0 and q == 0:
                @pl.when(k == 3)
                def _():
                    xcopy(0, 1).wait_recv()
                    forward(0, lambda e: xcopy(e, 1).start())

    def w_hops(k0, n, lo, hi):
        def body(t, _):
            w_hop(k0, n, t)
            return 0
        lax.fori_loop(lo, hi, body, 0)

    def load(i, slot):
        rows = pl.ds(pl.multiple_of(i * PIECE, PIECE), PIECE)
        return pltpu.make_async_copy(prior.at[rows], stage.at[slot], st_sem.at[slot])

    def take(i):
        slot = lax.rem(i, 2)
        load(i, slot).wait()
        for t in range(0, PIECE, 16):
            h, l = split(stage[slot, t:t + 16, :])
            rows = pl.ds(pl.multiple_of(i * PIECE + t, 16), 16)
            ph[rows, :] = h
            plo[rows, :] = l

        @pl.when(i + 2 < 16)
        def _():
            load(i + 2, slot).start()

    def spot(job):
        cols, rb, s, so, zo, j = job
        return pl.ds(cols[0], cols[1]), rb, s, so, zo, j

    def own(job, zz, cr):
        _, rb, s, _, _, _ = job
        return pl.ds(pl.multiple_of(rb + cr * 4 * s + zz * s, 16), s)

    def a_copy(job):
        cols, rb, s, so, zo, j = spot(job)
        return remote(part.at[pl.ds(pl.multiple_of(rb + (1 - core) * 4 * s, 16), 4 * s), cols],
                      sib.at[pl.ds(so, 4 * s), cols], j_send.at[j, 0], j_recv.at[j, 0], sibling)

    def b_copy(job, k):
        cols, rb, s, so, zo, j = spot(job)
        return remote(part.at[own(job, lax.rem(z + k, 4), core), cols],
                      zr.at[k - 1, pl.ds(zo, s), cols], j_send.at[j, k], j_recv.at[j, k], zpeer(k))

    def c_copy(job, k):
        cols, rb, s, so, zo, j = spot(job)
        o = own(job, z, core)
        return remote(full.at[o, cols], full.at[o, cols], j_send.at[j, 3 + k], j_recv.at[j, 3 + k],
                      zpeer(k) if k < 4 else sibling)

    def d_copy(job, k, cr):
        cols, rb, s, so, zo, j = spot(job)
        o = own(job, lax.rem(z + 4 - k, 4), cr)
        return remote(full.at[o, cols], full.at[o, cols], j_send.at[j, 7 + k], j_recv.at[j, 7 + k], sibling)

    def h_copy(job, half, zz, cr, dev, idx):
        cols, rb, s, so, zo, j = spot(job)
        o = pl.ds(pl.multiple_of(rb + cr * 4 * s + zz * s + half * (s // 2), 8), s // 2)
        return remote(full.at[o, cols], full.at[o, cols], j_send.at[j, idx], j_recv.at[j, idx], dev)

    def across(job, half):
        zz = lax.rem(z + (3 if half == 0 else 1), 4)
        return h_copy(job, half, zz, core, zpeer(1 if half == 0 else 3), 11 + half)

    def beside(job, half):
        return h_copy(job, half, lax.rem(z + 2, 4), core, sibling, 13 + half)

    def step_a(job):
        a_copy(job).start()

    def step_b(job):
        cols, rb, s, so, zo, j = spot(job)
        a_copy(job).wait_recv()

        def body(i, _):
            o = pl.ds(pl.multiple_of(rb + core * 4 * s + i * 32, 32), 32)
            part[o, cols] = part[o, cols] + sib[pl.ds(pl.multiple_of(so + i * 32, 32), 32), cols]
            return 0
        lax.fori_loop(0, s // 8, body, 0)
        for k in (2, 1, 3):
            b_copy(job, k).start()

    def step_c(job, nugget, relay=False):
        cols, rb, s, so, zo, j = spot(job)
        wide = job[0][1]
        for k in (1, 2, 3):
            b_copy(job, k).wait_recv()
        hx, hy = xyh[0:1, cols], xyh[1:2, cols]

        def body(i, _):
            first = rb + core * 4 * s + z * s + i * 32
            o = pl.ds(pl.multiple_of(first, 32), 32)
            t = pl.ds(pl.multiple_of(zo + i * 32, 32), 32)
            total = part[o, cols] + zr[0, t, cols] + (zr[1, t, cols] + zr[2, t, cols])
            dx = coords_t[o, 0:1] - hx
            dy = coords_t[o, 1:2] - hy
            scaled = root_three * jnp.sqrt(dx * dx + dy * dy) / lengthscale[...]
            val = variance[...] * (1.0 + scaled) * jnp.exp(-scaled)
            if nugget:
                ri = lax.broadcasted_iota(jnp.int32, (32, wide), 0) + first
                ci = lax.broadcasted_iota(jnp.int32, (32, wide), 1) + job[0][0]
                val = val + jnp.where(ri == ci, nugget_ref[...], 0.0)
            full[o, cols] = val - total
            return 0
        lax.fori_loop(0, s // 32, body, 0)
        for k in (1, 3, 4) if relay else (2, 1, 3, 4):
            c_copy(job, k).start()

    def step_d(job, relay=False):
        for k in (1, 3) if relay else (1, 3, 2):
            c_copy(job, k).wait_recv()
            if relay:
                across(job, 0 if k == 1 else 1).start()
            d_copy(job, k, core).start()

    def step_f(job):
        for half in (0, 1):
            across(job, half).wait_recv()
            beside(job, half).start()

    def step_e(job, relay=False):
        c_copy(job, 4).wait_recv()
        for k in (1, 3) if relay else (1, 2, 3):
            d_copy(job, k, 1 - core).wait_recv()
        if relay:
            for half in (0, 1):
                beside(job, half).wait_recv()

    def job_done(job, relay=False):
        a_copy(job).wait_send()
        for k in (1, 2, 3):
            b_copy(job, k).wait_send()
            if k != 2 or not relay:
                c_copy(job, k).wait_send()
                d_copy(job, k, core).wait_send()
        c_copy(job, 4).wait_send()
        if relay:
            for half in (0, 1):
                across(job, half).wait_send()
                beside(job, half).wait_send()

    def u_copy(i):
        cols = pl.ds(0, 768) if i == 0 else pl.ds(768, 256)
        return pltpu.make_async_copy(full.at[:, cols], u_out.at[:, cols], o_sem.at[i])

    load(0, 0).start()
    load(1, 1).start()
    coords_t[...] = jnp.concatenate([coords[...]] * 4, axis=0).T

    @pl.when(is_root)
    def _():
        xyh[0:2, :] = coords[:, 0:1024]

        def send(c, _):
            for q in range(4):
                root_send(q, lambda e: hcopy(q, e, c, prior).start())

            @pl.when(c == 1)
            def _():
                root_send(0, lambda e: xcopy(e, 0).start())
            return 0
        lax.fori_loop(0, CH, send, 0)

        def tk(i, _):
            take(i)
            return 0
        lax.fori_loop(0, 16, tk, 0)
        gram = [((256 * c, 256), 256 * c, 32 * (4 - c), 0, 0, c) for c in range(4)]
        rest = ((0, 1024), 1024, 64, 512, 128, 4)

        def blk(rb, n, c):
            cc = pl.ds(pl.multiple_of(c * 256, 256), 256)
            part[rb:rb + n, cc] = nt3(ph[rb:rb + n, :], plo[rb:rb + n, :], ph[cc, :], plo[cc, :])
        for c in range(4):
            blk(256 * c, 1024 - 256 * c, c)
            step_a(gram[c])
            if c:
                step_b(gram[c - 1])
        step_b(gram[3])
        step_c(gram[0], True)
        ch, cl = split(jnp.broadcast_to(carried[...], (16, 2048)))

        def pbody(c, _):
            cc = pl.ds(pl.multiple_of(c * 256, 256), 256)
            pj[0, :, cc] = nt3(ch, cl, ph[cc, :], plo[cc, :])[0:8]
            return 0
        lax.fori_loop(0, 4, pbody, 0)

        def pcopy(k):
            return remote(pj.at[0], pj.at[k], p_send.at[k - 1], p_recv.at[k - 1], {"depth": lax.rem(d + k, 8)})
        for k in range(1, 8):
            pcopy(k).start()
        step_c(gram[1], True)

        def rbody(i, _):
            r = pl.ds(pl.multiple_of(1024 + lax.div(i, 4) * 256, 256), 256)
            cc = pl.ds(pl.multiple_of(lax.rem(i, 4) * 256, 256), 256)
            part[r, cc] = nt3(ph[r, :], plo[r, :], ph[cc, :], plo[cc, :])
            return 0
        lax.fori_loop(0, 4, rbody, 0)
        step_d(gram[0])
        lax.fori_loop(4, 8, rbody, 0)
        step_a(rest)
        step_c(gram[2], True)
        n = 1024
        head[:, 0:n] = jnp.zeros((n, n), f32)

        def merge(c):
            step_e(gram[c])
            lo, hi = 256 * c, 256 * c + 256
            head[lo:n, lo:hi] = head[lo:n, lo:hi] + full[lo:n, lo:hi]
            if c < 3:
                t = full[hi:n, lo:hi].T
                head[lo:hi, hi:n] = head[lo:hi, hi:n] + t
                full[lo:hi, hi:n] = t
        merge(0)
        ri = lax.broadcasted_iota(jnp.int32, (B, n), 0)
        ci = lax.broadcasted_iota(jnp.int32, (B, n), 1)
        rows = lax.broadcasted_iota(jnp.int32, (n, 1), 0)

        def step(k, _):
            @pl.when(k == 1)
            def _():
                step_d(gram[1])
                step_c(gram[3], True)

            @pl.when(k == 2)
            def _():
                merge(1)
                step_d(gram[2])

            @pl.when(k == 3)
            def _():
                step_d(gram[3])
                step_b(rest)
                for i in range(1, 8):
                    pcopy(i).wait_recv()
                proj = functools.reduce(jnp.add, [pj[i] for i in range(8)])
                wbuf[1024:1032, :] = target[...] - proj
                root_send(0, lambda e: xcopy(e, 1).start())

            @pl.when(k == 4)
            def _():
                merge(2)

            @pl.when(k == 5)
            def _():
                step_c(rest, False)

            @pl.when(k == 6)
            def _():
                merge(3)

            @pl.when(k == 7)
            def _():
                step_d(rest)
            ks = pl.multiple_of(k * B, B)
            m = base(head[pl.ds(ks, B), pl.ds(ks, B)])
            inblk = (ci >= ks) & (ci < ks + B)
            row = jnp.where(inblk, (ci == ri + ks).astype(f32), head[pl.ds(ks, B), 0:n])
            r = mm(sl(m), sr(row))
            wbuf[pl.ds(ks, B), :] = jnp.where(ci < ks + B, r, 0.0)
            for q in range(4):
                root_send(q, lambda e: wcopy(q, e, k).start())

            @pl.when(k < 7)
            def _():
                rs = sr(r)
                mt = sr(m.T)
                act = rows >= ks + B
                gs = sl(jnp.where(act, mm(sl(head[:, pl.ds(ks, B)]), mt), 0.0))
                for i in range(1, 8):
                    zap = act[i * B:(i + 1) * B] & inblk
                    cur = jnp.where(zap, 0.0, head[i * B:(i + 1) * B, 0:n])
                    head[i * B:(i + 1) * B, 0:n] = cur - mm(gs[i * B:(i + 1) * B], rs)
            return 0
        lax.fori_loop(0, 8, step, 0)

        step_e(rest)
        u_copy(0).start()
        for job in gram + [rest]:
            job_done(job)
        for k in range(1, 8):
            pcopy(k).wait_send()

    @pl.when(jnp.logical_not(is_root))
    def _():
        jobs = [((128 * c, 128), 0, 192, 0, 0, c) for c in range(8)]

        def early(s, _):
            arrive(s)
            take(s)
            return 0
        lax.fori_loop(0, 16, early, 0)
        lead = 4 + D * (DEEP - 1)

        def block(m, hops=None):
            def cut(t, _):
                h, l = split(head[pl.ds(pl.multiple_of(m * 128 + t * 16, 16), 16), :])
                o = pl.ds(pl.multiple_of(t * 16, 16), 16)
                hb[o, :] = h
                hb[pl.ds(pl.multiple_of(128 + t * 16, 16), 16), :] = l
                return 0
            lax.fori_loop(0, 8, cut, 0)

            def piece(i, _):
                if m < 7:
                    arrive(lead + 4 * m + i)
                r = pl.ds(pl.multiple_of(i * 384, 384), 384)
                both = nt(ph[r, :], hb[...])
                low = nt(plo[r, :], hb[0:128, :])
                part[r, m * 128:m * 128 + 128] = both[:, 0:128] + (both[:, 128:256] + low)
                if hops is not None:
                    @pl.when(lax.rem(i, 2) == 1)
                    def _():
                        w_hop(0, 8, hops + lax.div(i, 2))
                return 0
            lax.fori_loop(0, 4, piece, 0)

        def tick(t):
            if t < 8:
                step_a(jobs[t])
            if 0 <= t - 1 < 8:
                step_b(jobs[t - 1])
            if 0 <= t - 2 < 8:
                step_c(jobs[t - 2], False, t - 2 < 6)
            if 0 <= t - 3 < 8:
                step_d(jobs[t - 3], t - 3 < 6)
            if 0 <= t - 4 < 6:
                step_f(jobs[t - 4])
        for m in range(8):
            block(m, 2 * (m - 5) if m >= 5 else None)
            tick(m)
        w_hops(0, 8, 6, 7)
        tick(8)
        w_hops(0, 8, 7, 9)
        tick(9)
        w_hops(0, 8, 9, 10)
        tick(10)
        for c in range(6):
            step_e(jobs[c], True)
        u_copy(0).start()
        w_hops(0, 8, 10, 12)
        for c in (6, 7):
            step_e(jobs[c], False)
        for q in range(4):
            for k in range(8):
                wsib(q, k, 1 - core).wait_recv()
        for c in range(8):
            job_done(jobs[c], c < 6)
        whole = wbuf.at[pl.ds(0, 512)]
        remote(whole, whole, ws_send, ws_recv.at[0, 0], sibling).wait_send()

    u_copy(1).start()
    wcp = pltpu.make_async_copy(wbuf, w_out, o_sem.at[2])
    wcp.start()
    for (q, e), has in sends.items():
        @pl.when(has)
        def _():
            ref = head.at[pl.ds(0, 256)]
            remote(ref, ref, head_send.at[q, e], head_recv.at[0, 0], nbr[e]).wait_send()
            ref = wbuf.at[pl.ds(0, 128)]
            remote(ref, ref, w_send.at[q, e], w_recv.at[0, 0], nbr[e]).wait_send()
            if q == 0:
                xcopy(e, 0).wait_send()
                xcopy(e, 1).wait_send()
    u_copy(0).wait()
    u_copy(1).wait()
    wcp.wait()


def gather_and_factor(prior, coords, carried, target, scalars):
    vm = pl.BlockSpec(memory_space=pltpu.VMEM)
    dma = pltpu.SemaphoreType.DMA
    bf = jnp.bfloat16
    return pl.pallas_call(
        kernel,
        out_shape=(jax.ShapeDtypeStruct((1536, 1024), f32), jax.ShapeDtypeStruct((1032, 1024), f32)),
        in_specs=[pl.BlockSpec(memory_space=pl.ANY), vm, vm, vm, vm, vm, vm],
        out_specs=(pl.BlockSpec(memory_space=pl.ANY), pl.BlockSpec(memory_space=pl.ANY)),
        scratch_shapes=[
            pltpu.VMEM((1536, 8), f32),
            pltpu.VMEM((1024, 2048), f32),
            pltpu.VMEM((1536, 2048), bf), pltpu.VMEM((1536, 2048), bf),
            pltpu.VMEM((256, 2048), bf),
            pltpu.VMEM((1536, 1024), f32), pltpu.VMEM((768, 1024), f32), pltpu.VMEM((3, 192, 1024), f32),
            pltpu.VMEM((1536, 1024), f32), pltpu.VMEM((1032, 1024), f32), pltpu.VMEM((2, PIECE, 2048), f32),
            pltpu.VMEM((8, 1024), f32), pltpu.VMEM((8, 8, 1024), f32),
            dma((4, 4)), dma((4, CH)), dma((4, 4)), dma((4, 8)), dma, dma((4, 8)), dma((2, 4)), dma((2,)),
            dma((8, 15)), dma((8, 15)), dma((7,)), dma((7,)), dma((2,)), dma((3,)),
        ],
        compiler_params=pltpu.CompilerParams(collective_id=1, has_side_effects=True, vmem_limit_bytes=60 << 20),
    )(prior, coords, carried[None, :], target[None, :], *[v.reshape(1, 1) for v in scalars])


def panel_kernel(u, w, out, sol, wh, wl):
    @pl.when(pl.program_id(0) == 0)
    def _():
        def cut(t, _):
            o = pl.ds(pl.multiple_of(t * 16, 16), 16)
            h, l = split(w[o, :])
            wh[o, :] = h
            wl[o, :] = l
            return 0
        lax.fori_loop(0, 64, cut, 0)
        rh, rl = split(jnp.concatenate([w[1024:1032, :]] * 2, axis=0))
        for j in range(4):
            o = slice(256 * j, 256 * j + 256)
            sol[:, o] = nt3(rh, rl, wh[o, :], wl[o, :])[0:1]
    uh, ul = split(u[...])
    for j in range(4):
        o, n = slice(256 * j, 256 * j + 256), 256 * j + 256
        out[:, o] = nt3(uh[:, :n], ul[:, :n], wh[o, :n], wl[o, :n])


def panel_product(update, inverse):
    m = 384
    return pl.pallas_call(
        panel_kernel,
        grid=(1536 // m,),
        out_shape=(jax.ShapeDtypeStruct((1536, 1024), f32), jax.ShapeDtypeStruct((1, 1024), f32)),
        in_specs=[pl.BlockSpec((m, 1024), lambda i: (i, 0)), pl.BlockSpec((1032, 1024), lambda i: (0, 0))],
        out_specs=(pl.BlockSpec((m, 1024), lambda i: (i, 0)), pl.BlockSpec((1, 1024), lambda i: (0, 0))),
        scratch_shapes=[pltpu.VMEM((1024, 1024), jnp.bfloat16)] * 2,
        compiler_params=pltpu.CompilerParams(vmem_limit_bytes=63 << 20),
    )(update, inverse)


def local(coords, prior, target, carried, variance, lengthscale, nugget):
    update, inverse = gather_and_factor(prior, coords, carried, target, (variance, lengthscale, nugget))
    panels, solved = panel_product(update, inverse)
    return (panels, solved.reshape(1024))


def solution(mesh):
    return jax.shard_map(
        local,
        mesh=mesh,
        in_specs=(
            P(None, ("row", "col")),
            P(("row", "col"), "depth"),
            P(),
            P("depth"),
            P(),
            P(),
            P(),
        ),
        out_specs=(P(("row", "col"), None), P()),
        check_vma=False,
    )
```

```python
import functools

import jax
import jax.numpy as jnp
from jax import lax
from jax.experimental import pallas as pl
from jax.experimental.pallas import tpu as pltpu
from jax.sharding import PartitionSpec as P

f32 = jnp.float32
MESH = pl.DeviceIdType.MESH
B = 128
root_three = 1.7320508075688772


def split(x):
    hi = x.astype(jnp.bfloat16)
    return hi, (x - hi.astype(f32)).astype(jnp.bfloat16)


def iota8():
    shape = (8, B)
    return lax.broadcasted_iota(jnp.int32, shape, 0), lax.broadcasted_iota(jnp.int32, shape, 1)

def base(x, b=32):
    n=B; row8,col8=iota8()
    T=n//8; nt=b//8
    X=[x[8*t:8*t+8] for t in range(T)]
    out=[]
    for blk in range(n//b):
        c0=blk*b; t0=c0//8
        C=[[jnp.broadcast_to(X[t0+t][:,c0+k:c0+k+1],(8,n)) for k in range(8*t+8)] for t in range(nt)]
        inb=(col8>=c0)&(col8<c0+b)
        E=[jnp.where(inb,(col8==row8+(c0+8*t)).astype(f32),X[t0+t]) for t in range(nt)]
        scale=[None]*nt
        for j in range(b):
            tj,sj=divmod(j,8)
            p=C[tj][j][sj:sj+1,:]
            pinv=1.0/p
            rs=lax.rsqrt(p)
            scale[tj]=jnp.broadcast_to(rs,(8,n)) if sj==0 else jnp.where(row8==sj,rs,scale[tj])
            er=E[tj][sj:sj+1,:]*pinv
            rk={}
            for k in range(j+1,b):
                tk,sk=divmod(k,8)
                rk[k]=C[tk][j][sk:sk+1,:]*pinv
            for t in range(tj,nt):
                c=C[t][j]
                for k in range(j+1,8*t+8):
                    C[t][k]=C[t][k]-c*rk[k]
                ce=jnp.where(row8>sj,c,0.0) if t==tj else c
                if not (t==tj and sj==7):
                    E[t]=E[t]-ce*er
        U=[E[t]*scale[t] for t in range(nt)]
        out+=U
        if c0+b<n:
            u=jnp.concatenate(U,axis=0)
            at=u.T[c0+b:]
            ah,al=split(at); bh,bl=split(u)
            l=jnp.concatenate([ah,al,ah],axis=1); r=jnp.concatenate([bh,bh,bl],axis=0)
            d=jnp.dot(l,r,preferred_element_type=f32)
            for t in range(t0+nt,T):
                o=8*t-(c0+b)
                X[t]=jnp.where(inb,0.0,X[t])-d[o:o+8]
    w=jnp.concatenate(out,axis=0)
    rr=lax.broadcasted_iota(jnp.int32,(n,n),0); cc=lax.broadcasted_iota(jnp.int32,(n,n),1)
    return jnp.where(cc<=rr,w,0.0)


WAY_IN = {(0, 1): 0, (3, 0): 2, (0, 3): 0, (1, 0): 2, (0, 2): 0, (2, 0): 2, (1, 1): 2, (3, 1): 1, (3, 3): 3,
          (1, 3): 2, (1, 2): 2, (2, 1): 1, (3, 2): 3, (2, 3): 2, (2, 2): 1}
STEP = ((1, 0), (0, 1), (-1, 0), (0, -1))

def tree_kids():
    kids = [[[] for _ in range(4)] for _ in range(4)]
    for node, way in WAY_IN.items():
        for q in range(4):
            x, y = node
            for _ in range(q):
                x, y = (-y) % 4, x
            e = (way + q) % 4
            kids[q][e].append((x - STEP[e][0]) % 4 + 4 * ((y - STEP[e][1]) % 4))
    return kids
KIDS = tree_kids()

def tree_depths():
    out = [[0] * 16 for _ in range(4)]
    for node in WAY_IN:
        u, k = node, 0
        while u != (0, 0):
            s = STEP[WAY_IN[u]]
            u, k = ((u[0] - s[0]) % 4, (u[1] - s[1]) % 4), k + 1
        x, y = node
        for q in range(4):
            out[q][x + 4 * y] = k
            x, y = (-y) % 4, x
    return out
DEPTH = tree_depths()


R = 8
D = 3
CH = 256 // R
DEEP = 5
PIECE = 96


def sl(a):
    h, l = split(a)
    return jnp.concatenate([h, l, h], axis=1)


def sr(b):
    h, l = split(b)
    return jnp.concatenate([h, h, l], axis=0)


def mm(left, right):
    return jnp.dot(left, right, preferred_element_type=f32)


def nt(left, right):
    return lax.dot_general(left, right, (((1,), (1,)), ((), ())), preferred_element_type=f32)


def nt3(lh, ll, rh, rl):
    return nt(lh, rh) + (nt(ll, rh) + nt(lh, rl))


def kernel(prior, coords, carried, target, variance, lengthscale, nugget_ref, u_out, w_out,
           coords_t, head, ph, plo, hb, part, sib, zr, full, wbuf, stage, xyh, pj,
           head_send, head_recv, w_send, w_recv, ws_send, ws_recv, x_send, x_recv,
           j_send, j_recv, p_send, p_recv, st_sem, o_sem):
    x, y, d = lax.axis_index("col"), lax.axis_index("row"), lax.axis_index("depth")
    z, core = lax.div(d, 2), lax.rem(d, 2)
    node = x + 4 * y
    nbr = [{"col": lax.rem(x + 4 + sx, 4), "row": lax.rem(y + 4 + sy, 4)} for sx, sy in STEP]
    sibling = {"depth": 2 * z + 1 - core}
    is_root = node == 0

    def zpeer(k):
        return {"depth": 2 * lax.rem(z + k, 4) + core}

    def remote(src, dst, ss, rs, dev):
        return pltpu.make_async_remote_copy(
            src_ref=src, dst_ref=dst, send_sem=ss, recv_sem=rs, device_id=dev, device_id_type=MESH)

    sends = {}
    for q in range(4):
        for e in range(4):
            if KIDS[q][e]:
                sends[q, e] = functools.reduce(jnp.logical_or, [node == k for k in KIDS[q][e]])
    depth = [sum(jnp.where(node == v, DEPTH[q][v], 0) for v in range(1, 16)) for q in range(4)]

    barrier = pltpu.get_barrier_semaphore()
    for e in range(4):
        pl.semaphore_signal(barrier, inc=1, device_id=nbr[e], device_id_type=MESH)
    for k in range(1, 8):
        pl.semaphore_signal(barrier, inc=1, device_id={"depth": lax.rem(d + k, 8)}, device_id_type=MESH)
    pl.semaphore_wait(barrier, 11)

    def hrows(q, c):
        return pl.ds(pl.multiple_of((c * 4 + q) * R, R), R)

    def hcopy(q, e, c, src):
        return remote(src.at[hrows(q, c)], head.at[hrows(q, c)], head_send.at[q, e], head_recv.at[q, c], nbr[e])

    def wrows(q, k, cr):
        return pl.ds(pl.multiple_of(k * B + cr * 64 + q * 16, 16), 16)

    def wcopy(q, e, k):
        r = wrows(q, k, core)
        return remote(wbuf.at[r], wbuf.at[r], w_send.at[q, e], w_recv.at[q, k], nbr[e])

    def wsib(q, k, cr):
        r = wrows(q, k, cr)
        return remote(wbuf.at[r], wbuf.at[r], ws_send, ws_recv.at[q, k], sibling)

    def xcopy(e, i):
        ref = xyh if i == 0 else wbuf.at[pl.ds(1024, 8)]
        return remote(ref, ref, x_send.at[i, e], x_recv.at[i], nbr[e])

    def forward(q, start):
        for e in range(4):
            if (q, e) in sends and any(k != 0 for k in KIDS[q][e]):
                @pl.when(sends[q, e])
                def _():
                    start(e)

    def root_send(q, start):
        for e in range(4):
            if (q, e) in sends and 0 in KIDS[q][e]:
                start(e)

    def arrive(s):
        for q in range(4):
            c = s - D * (depth[q] - 1)

            @pl.when((c >= 0) & (c < CH))
            def _():
                hcopy(q, 0, c, head).wait_recv()
                forward(q, lambda e: hcopy(q, e, c, head).start())
            if q == 0:
                @pl.when(c == 1)
                def _():
                    xcopy(0, 0).wait_recv()
                    forward(0, lambda e: xcopy(e, 0).start())

    def w_hop(k0, n, t):
        for q in range(4):
            k = k0 + t - (depth[q] - 1)

            @pl.when((k >= k0) & (k < k0 + n))
            def _():
                wcopy(q, 0, k).wait_recv()
                forward(q, lambda e: wcopy(q, e, k).start())
                wsib(q, k, core).start()
            if k0 == 0 and q == 0:
                @pl.when(k == 3)
                def _():
                    xcopy(0, 1).wait_recv()
                    forward(0, lambda e: xcopy(e, 1).start())

    def w_hops(k0, n, lo, hi):
        def body(t, _):
            w_hop(k0, n, t)
            return 0
        lax.fori_loop(lo, hi, body, 0)

    def load(i, slot):
        rows = pl.ds(pl.multiple_of(i * PIECE, PIECE), PIECE)
        return pltpu.make_async_copy(prior.at[rows], stage.at[slot], st_sem.at[slot])

    def take(i):
        slot = lax.rem(i, 2)
        load(i, slot).wait()
        for t in range(0, PIECE, 16):
            h, l = split(stage[slot, t:t + 16, :])
            rows = pl.ds(pl.multiple_of(i * PIECE + t, 16), 16)
            ph[rows, :] = h
            plo[rows, :] = l

        @pl.when(i + 2 < 16)
        def _():
            load(i + 2, slot).start()

    def spot(job):
        cols, rb, s, so, zo, j = job
        return pl.ds(cols[0], cols[1]), rb, s, so, zo, j

    def own(job, zz, cr):
        _, rb, s, _, _, _ = job
        return pl.ds(pl.multiple_of(rb + cr * 4 * s + zz * s, 16), s)

    def a_copy(job):
        cols, rb, s, so, zo, j = spot(job)
        return remote(part.at[pl.ds(pl.multiple_of(rb + (1 - core) * 4 * s, 16), 4 * s), cols],
                      sib.at[pl.ds(so, 4 * s), cols], j_send.at[j, 0], j_recv.at[j, 0], sibling)

    def b_copy(job, k):
        cols, rb, s, so, zo, j = spot(job)
        return remote(part.at[own(job, lax.rem(z + k, 4), core), cols],
                      zr.at[k - 1, pl.ds(zo, s), cols], j_send.at[j, k], j_recv.at[j, k], zpeer(k))

    def c_copy(job, k):
        cols, rb, s, so, zo, j = spot(job)
        o = own(job, z, core)
        return remote(full.at[o, cols], full.at[o, cols], j_send.at[j, 3 + k], j_recv.at[j, 3 + k],
                      zpeer(k) if k < 4 else sibling)

    def d_copy(job, k, cr):
        cols, rb, s, so, zo, j = spot(job)
        o = own(job, lax.rem(z + 4 - k, 4), cr)
        return remote(full.at[o, cols], full.at[o, cols], j_send.at[j, 7 + k], j_recv.at[j, 7 + k], sibling)

    def h_copy(job, half, zz, cr, dev, idx):
        cols, rb, s, so, zo, j = spot(job)
        o = pl.ds(pl.multiple_of(rb + cr * 4 * s + zz * s + half * (s // 2), 8), s // 2)
        return remote(full.at[o, cols], full.at[o, cols], j_send.at[j, idx], j_recv.at[j, idx], dev)

    def across(job, half):
        zz = lax.rem(z + (3 if half == 0 else 1), 4)
        return h_copy(job, half, zz, core, zpeer(1 if half == 0 else 3), 11 + half)

    def beside(job, half):
        return h_copy(job, half, lax.rem(z + 2, 4), core, sibling, 13 + half)

    def step_a(job):
        a_copy(job).start()

    def step_b(job):
        cols, rb, s, so, zo, j = spot(job)
        a_copy(job).wait_recv()

        def body(i, _):
            o = pl.ds(pl.multiple_of(rb + core * 4 * s + i * 32, 32), 32)
            part[o, cols] = part[o, cols] + sib[pl.ds(pl.multiple_of(so + i * 32, 32), 32), cols]
            return 0
        lax.fori_loop(0, s // 8, body, 0)
        for k in (2, 1, 3):
            b_copy(job, k).start()

    def step_c(job, nugget, relay=False):
        cols, rb, s, so, zo, j = spot(job)
        wide = job[0][1]
        for k in (1, 2, 3):
            b_copy(job, k).wait_recv()
        hx, hy = xyh[0:1, cols], xyh[1:2, cols]

        def body(i, _):
            first = rb + core * 4 * s + z * s + i * 32
            o = pl.ds(pl.multiple_of(first, 32), 32)
            t = pl.ds(pl.multiple_of(zo + i * 32, 32), 32)
            total = part[o, cols] + zr[0, t, cols] + (zr[1, t, cols] + zr[2, t, cols])
            dx = coords_t[o, 0:1] - hx
            dy = coords_t[o, 1:2] - hy
            scaled = root_three * jnp.sqrt(dx * dx + dy * dy) / lengthscale[...]
            val = variance[...] * (1.0 + scaled) * jnp.exp(-scaled)
            if nugget:
                ri = lax.broadcasted_iota(jnp.int32, (32, wide), 0) + first
                ci = lax.broadcasted_iota(jnp.int32, (32, wide), 1) + job[0][0]
                val = val + jnp.where(ri == ci, nugget_ref[...], 0.0)
            full[o, cols] = val - total
            return 0
        lax.fori_loop(0, s // 32, body, 0)
        for k in (1, 3, 4) if relay else (2, 1, 3, 4):
            c_copy(job, k).start()

    def step_d(job, relay=False):
        for k in (1, 3) if relay else (1, 3, 2):
            c_copy(job, k).wait_recv()
            if relay:
                across(job, 0 if k == 1 else 1).start()
            d_copy(job, k, core).start()

    def step_f(job):
        for half in (0, 1):
            across(job, half).wait_recv()
            beside(job, half).start()

    def step_e(job, relay=False):
        c_copy(job, 4).wait_recv()
        for k in (1, 3) if relay else (1, 2, 3):
            d_copy(job, k, 1 - core).wait_recv()
        if relay:
            for half in (0, 1):
                beside(job, half).wait_recv()

    def job_done(job, relay=False):
        a_copy(job).wait_send()
        for k in (1, 2, 3):
            b_copy(job, k).wait_send()
            if k != 2 or not relay:
                c_copy(job, k).wait_send()
                d_copy(job, k, core).wait_send()
        c_copy(job, 4).wait_send()
        if relay:
            for half in (0, 1):
                across(job, half).wait_send()
                beside(job, half).wait_send()

    def u_copy(i):
        cols = pl.ds(0, 768) if i == 0 else pl.ds(768, 256)
        return pltpu.make_async_copy(full.at[:, cols], u_out.at[:, cols], o_sem.at[i])

    load(0, 0).start()
    load(1, 1).start()
    coords_t[...] = jnp.concatenate([coords[...]] * 4, axis=0).T

    @pl.when(is_root)
    def _():
        xyh[0:2, :] = coords[:, 0:1024]

        def send(c, _):
            for q in range(4):
                root_send(q, lambda e: hcopy(q, e, c, prior).start())

            @pl.when(c == 1)
            def _():
                root_send(0, lambda e: xcopy(e, 0).start())
            return 0
        lax.fori_loop(0, CH, send, 0)

        def tk(i, _):
            take(i)
            return 0
        lax.fori_loop(0, 16, tk, 0)
        gram = [((256 * c, 256), 256 * c, 32 * (4 - c), 0, 0, c) for c in range(4)]
        rest = ((0, 1024), 1024, 64, 512, 128, 4)

        def blk(rb, n, c):
            cc = pl.ds(pl.multiple_of(c * 256, 256), 256)
            part[rb:rb + n, cc] = nt3(ph[rb:rb + n, :], plo[rb:rb + n, :], ph[cc, :], plo[cc, :])
        for c in range(4):
            blk(256 * c, 1024 - 256 * c, c)
            step_a(gram[c])
            if c:
                step_b(gram[c - 1])
        step_b(gram[3])
        step_c(gram[0], True)
        ch, cl = split(jnp.broadcast_to(carried[...], (16, 2048)))

        def pbody(c, _):
            cc = pl.ds(pl.multiple_of(c * 256, 256), 256)
            pj[0, :, cc] = nt3(ch, cl, ph[cc, :], plo[cc, :])[0:8]
            return 0
        lax.fori_loop(0, 4, pbody, 0)

        def pcopy(k):
            return remote(pj.at[0], pj.at[k], p_send.at[k - 1], p_recv.at[k - 1], {"depth": lax.rem(d + k, 8)})
        for k in range(1, 8):
            pcopy(k).start()
        step_c(gram[1], True)

        def rbody(i, _):
            r = pl.ds(1024, 512)
            cc = pl.ds(pl.multiple_of(i * 256, 256), 256)
            part[r, cc] = nt3(ph[r, :], plo[r, :], ph[cc, :], plo[cc, :])
            return 0
        lax.fori_loop(0, 2, rbody, 0)
        step_d(gram[0])
        lax.fori_loop(2, 4, rbody, 0)
        step_a(rest)
        step_c(gram[2], True)
        n = 1024
        head[:, 0:n] = jnp.zeros((n, n), f32)

        def merge(c):
            step_e(gram[c])
            lo, hi = 256 * c, 256 * c + 256
            head[lo:n, lo:hi] = head[lo:n, lo:hi] + full[lo:n, lo:hi]
            if c < 3:
                t = full[hi:n, lo:hi].T
                head[lo:hi, hi:n] = head[lo:hi, hi:n] + t
                full[lo:hi, hi:n] = t
        merge(0)
        ri = lax.broadcasted_iota(jnp.int32, (B, n), 0)
        ci = lax.broadcasted_iota(jnp.int32, (B, n), 1)
        rows = lax.broadcasted_iota(jnp.int32, (n, 1), 0)

        def step(k, _):
            @pl.when(k == 1)
            def _():
                step_d(gram[1])
                step_c(gram[3], True)

            @pl.when(k == 2)
            def _():
                merge(1)
                step_d(gram[2])

            @pl.when(k == 3)
            def _():
                step_d(gram[3])
                step_b(rest)
                for i in range(1, 8):
                    pcopy(i).wait_recv()
                proj = functools.reduce(jnp.add, [pj[i] for i in range(8)])
                wbuf[1024:1032, :] = target[...] - proj
                root_send(0, lambda e: xcopy(e, 1).start())

            @pl.when(k == 4)
            def _():
                merge(2)

            @pl.when(k == 5)
            def _():
                step_c(rest, False)

            @pl.when(k == 6)
            def _():
                merge(3)

            @pl.when(k == 7)
            def _():
                step_d(rest)
            ks = pl.multiple_of(k * B, B)
            m = base(head[pl.ds(ks, B), pl.ds(ks, B)])
            inblk = (ci >= ks) & (ci < ks + B)
            row = jnp.where(inblk, (ci == ri + ks).astype(f32), head[pl.ds(ks, B), 0:n])
            r = mm(sl(m), sr(row))
            wbuf[pl.ds(ks, B), :] = jnp.where(ci < ks + B, r, 0.0)
            for q in range(4):
                root_send(q, lambda e: wcopy(q, e, k).start())

            @pl.when(k < 7)
            def _():
                rs = sr(r)
                mt = sr(m.T)

                def below(i0, i1):
                    act = rows[i0 * B:i1 * B] >= ks + B
                    gs = sl(jnp.where(act, mm(sl(head[i0 * B:i1 * B, pl.ds(ks, B)]), mt), 0.0))
                    for i in range(i0, i1):
                        o = slice((i - i0) * B, (i - i0 + 1) * B)
                        cur = jnp.where(act[o] & inblk, 0.0, head[i * B:(i + 1) * B, 0:n])
                        head[i * B:(i + 1) * B, 0:n] = cur - mm(gs[o], rs)

                @pl.when(k < 3)
                def _():
                    below(1, 4)
                below(4, 8)
            return 0
        lax.fori_loop(0, 8, step, 0)

        step_e(rest)
        u_copy(0).start()
        for job in gram + [rest]:
            job_done(job)
        for k in range(1, 8):
            pcopy(k).wait_send()

    @pl.when(jnp.logical_not(is_root))
    def _():
        jobs = [((128 * c, 128), 0, 192, 0, 0, c) for c in range(8)]

        def early(s, _):
            arrive(s)
            take(s)
            return 0
        lax.fori_loop(0, 16, early, 0)
        lead = 4 + D * (DEEP - 1)

        def block(m, hops=None):
            def cut(t, _):
                h, l = split(head[pl.ds(pl.multiple_of(m * 128 + t * 16, 16), 16), :])
                o = pl.ds(pl.multiple_of(t * 16, 16), 16)
                hb[o, :] = h
                hb[pl.ds(pl.multiple_of(128 + t * 16, 16), 16), :] = l
                return 0
            lax.fori_loop(0, 8, cut, 0)

            def piece(i, _):
                if m < 7:
                    arrive(lead + 4 * m + i)
                r = pl.ds(pl.multiple_of(i * 384, 384), 384)
                both = nt(ph[r, :], hb[...])
                low = nt(plo[r, :], hb[0:128, :])
                part[r, m * 128:m * 128 + 128] = both[:, 0:128] + (both[:, 128:256] + low)
                if hops is not None:
                    @pl.when(lax.rem(i, 2) == 1)
                    def _():
                        w_hop(0, 8, hops + lax.div(i, 2))
                return 0
            lax.fori_loop(0, 4, piece, 0)

        def tick(t):
            if t < 8:
                step_a(jobs[t])
            if 0 <= t - 1 < 8:
                step_b(jobs[t - 1])
            if 0 <= t - 2 < 8:
                step_c(jobs[t - 2], False, t - 2 < 6)
            if 0 <= t - 3 < 8:
                step_d(jobs[t - 3], t - 3 < 6)
            if 0 <= t - 4 < 6:
                step_f(jobs[t - 4])
        for m in range(8):
            block(m, 2 * (m - 5) if m >= 5 else None)
            tick(m)
        w_hops(0, 8, 6, 7)
        tick(8)
        w_hops(0, 8, 7, 9)
        tick(9)
        w_hops(0, 8, 9, 11)
        tick(10)
        w_hops(0, 8, 11, 12)
        for c in range(6):
            step_e(jobs[c], True)
        u_copy(0).start()
        for c in (6, 7):
            step_e(jobs[c], False)
        for q in range(4):
            for k in range(8):
                wsib(q, k, 1 - core).wait_recv()
        for c in range(8):
            job_done(jobs[c], c < 6)
        whole = wbuf.at[pl.ds(0, 512)]
        remote(whole, whole, ws_send, ws_recv.at[0, 0], sibling).wait_send()

    u_copy(1).start()
    wcp = pltpu.make_async_copy(wbuf, w_out, o_sem.at[2])
    wcp.start()
    for (q, e), has in sends.items():
        @pl.when(has)
        def _():
            ref = head.at[pl.ds(0, 256)]
            remote(ref, ref, head_send.at[q, e], head_recv.at[0, 0], nbr[e]).wait_send()
            ref = wbuf.at[pl.ds(0, 128)]
            remote(ref, ref, w_send.at[q, e], w_recv.at[0, 0], nbr[e]).wait_send()
            if q == 0:
                xcopy(e, 0).wait_send()
                xcopy(e, 1).wait_send()
    u_copy(0).wait()
    u_copy(1).wait()
    wcp.wait()


def gather_and_factor(prior, coords, carried, target, scalars):
    vm = pl.BlockSpec(memory_space=pltpu.VMEM)
    dma = pltpu.SemaphoreType.DMA
    bf = jnp.bfloat16
    return pl.pallas_call(
        kernel,
        out_shape=(jax.ShapeDtypeStruct((1536, 1024), f32), jax.ShapeDtypeStruct((1032, 1024), f32)),
        in_specs=[pl.BlockSpec(memory_space=pl.ANY), vm, vm, vm, vm, vm, vm],
        out_specs=(pl.BlockSpec(memory_space=pl.ANY), pl.BlockSpec(memory_space=pl.ANY)),
        scratch_shapes=[
            pltpu.VMEM((1536, 8), f32),
            pltpu.VMEM((1024, 2048), f32),
            pltpu.VMEM((1536, 2048), bf), pltpu.VMEM((1536, 2048), bf),
            pltpu.VMEM((256, 2048), bf),
            pltpu.VMEM((1536, 1024), f32), pltpu.VMEM((768, 1024), f32), pltpu.VMEM((3, 192, 1024), f32),
            pltpu.VMEM((1536, 1024), f32), pltpu.VMEM((1032, 1024), f32), pltpu.VMEM((2, PIECE, 2048), f32),
            pltpu.VMEM((8, 1024), f32), pltpu.VMEM((8, 8, 1024), f32),
            dma((4, 4)), dma((4, CH)), dma((4, 4)), dma((4, 8)), dma, dma((4, 8)), dma((2, 4)), dma((2,)),
            dma((8, 15)), dma((8, 15)), dma((7,)), dma((7,)), dma((2,)), dma((3,)),
        ],
        compiler_params=pltpu.CompilerParams(collective_id=1, has_side_effects=True, vmem_limit_bytes=60 << 20),
    )(prior, coords, carried[None, :], target[None, :], *[v.reshape(1, 1) for v in scalars])


def panel_kernel(u, w, out, sol, wh, wl):
    @pl.when(pl.program_id(0) == 0)
    def _():
        def cut(t, _):
            o = pl.ds(pl.multiple_of(t * 16, 16), 16)
            h, l = split(w[o, :])
            wh[o, :] = h
            wl[o, :] = l
            return 0
        lax.fori_loop(0, 64, cut, 0)
        rh, rl = split(jnp.concatenate([w[1024:1032, :]] * 2, axis=0))
        for j in range(4):
            o = slice(256 * j, 256 * j + 256)
            sol[:, o] = nt3(rh, rl, wh[o, :], wl[o, :])[0:1]
    uh, ul = split(u[...])
    for j in range(4):
        o, n = slice(256 * j, 256 * j + 256), 256 * j + 256
        out[:, o] = nt3(uh[:, :n], ul[:, :n], wh[o, :n], wl[o, :n])


def panel_product(update, inverse):
    m = 384
    return pl.pallas_call(
        panel_kernel,
        grid=(1536 // m,),
        out_shape=(jax.ShapeDtypeStruct((1536, 1024), f32), jax.ShapeDtypeStruct((1, 1024), f32)),
        in_specs=[pl.BlockSpec((m, 1024), lambda i: (i, 0)), pl.BlockSpec((1032, 1024), lambda i: (0, 0))],
        out_specs=(pl.BlockSpec((m, 1024), lambda i: (i, 0)), pl.BlockSpec((1, 1024), lambda i: (0, 0))),
        scratch_shapes=[pltpu.VMEM((1024, 1024), jnp.bfloat16)] * 2,
        compiler_params=pltpu.CompilerParams(vmem_limit_bytes=63 << 20),
    )(update, inverse)


def local(coords, prior, target, carried, variance, lengthscale, nugget):
    update, inverse = gather_and_factor(prior, coords, carried, target, (variance, lengthscale, nugget))
    panels, solved = panel_product(update, inverse)
    return (panels, solved.reshape(1024))


def solution(mesh):
    return jax.shard_map(
        local,
        mesh=mesh,
        in_specs=(
            P(None, ("row", "col")),
            P(("row", "col"), "depth"),
            P(),
            P("depth"),
            P(),
            P(),
            P(),
        ),
        out_specs=(P(("row", "col"), None), P()),
        check_vma=False,
    )
```
